256 devices in a mesh: section: 16 (over z, core), ep: 16 (over y, x).
Axes of the slice: x: 4, y: 4, z: 8, core: 2. Of those that a mesh axis runs over, the one named last changes fastest.
Arguments:
- states: bfloat16 [4096, 3072], P(('section', 'ep')), may hold values from -6 to 6
- entering: bfloat16 [256, 3072], P('ep'), may hold values from -6 to 6
- seq_lens: int32 [17, 256], replicated, may hold values from 1 to 16, 2048 in all within a row
- routes: int32 [16, 2, 256, 2], P('section', None, 'ep'), may hold values from 0 to 7, all different within a row; in each aligned block of 16 rows (0 to 15, 16 to 31, ..., all dimensions but the last counted through in order) at most 8 rows name the same one
- attn_norm: bfloat16 [16, 3072], P('section'), may hold values from 0.099609375 to 1.8984375
- ffn_norm: bfloat16 [16, 3072], P('section'), may hold values from 0.099609375 to 1.8984375
- wq: bfloat16 [16, 3072, 4096], P('section', None, 'ep'), may hold values from -0.109375 to 0.109375
- wk: bfloat16 [16, 3072, 1024], P('section', None, 'ep'), may hold values from -0.109375 to 0.109375
- wv: bfloat16 [16, 3072, 1024], P('section', None, 'ep'), may hold values from -0.109375 to 0.109375
- wo: bfloat16 [16, 4096, 3072], P('section', 'ep'), may hold values from -0.09375 to 0.09375
- router: bfloat16 [16, 3072, 8], P('section'), may hold values from -0.21875 to 0.21875
- w_gate: bfloat16 [16, 3072, 7168], P('section', None, 'ep'), may hold values from -0.109375 to 0.109375
- w_up: bfloat16 [16, 3072, 7168], P('section', None, 'ep'), may hold values from -0.109375 to 0.109375
- w_down: bfloat16 [16, 7168, 3072], P('section', 'ep'), may hold values from -0.125 to 0.125
- cache_k: bfloat16 [16, 2, 256, 8, 16, 128], P('section', None, 'ep'), may hold values from -127 to 127, as said below
- cache_v: bfloat16 [16, 2, 256, 8, 16, 128], P('section', None, 'ep'), may hold values from -127 to 127, as said below
- k_scale: float32 [16, 2, 256, 8, 4], P('section', None, 'ep'), may hold values from 0.004 to 2.4
- v_scale: float32 [16, 2, 256, 8, 4], P('section', None, 'ep'), may hold values from 0.004 to 0.04
Outputs:
- advanced: bfloat16 [4096, 3072], P(('section', 'ep'))
The draws below stay inside these ranges and needn't reach their ends.
Inputs may be any that keep to these rules, and one draw needn't show every extreme that they name: `seq_lens`: each row holds 256 lengths; the longest is exactly 16. `routes`: the two ids of a token differ. In the rows of one device (aligned blocks of 16 tokens of a section and step) no expert is named by more than 8 tokens. `cache_k`: whole numbers. `cache_v`: whole numbers.
All inputs are finite; a program needn't handle non-finite values.
Results may differ from the reference program's by a relative error of at most 0.033.
Values may be sent and summed in bfloat16 or wider, within the bound.
No kernel may reach another device: no remote copies, remote signals or barrier semaphores. Data moves between devices by JAX's collectives and lax.ppermute only.
A program may use at most 128 MiB of HBM per device.

```python
import math
import jax
import jax.numpy as jnp
import numpy as np
from jax import lax

D = 3072
QH = 32
KVH = 8
HD = 128
EXPERTS = 8
EXP_WIN = 1
FFE = 7168
TOK_DEV = 16
LEN = 16
BLK = 4
TICKS = 2
SECTIONS = 16
MICRO = 17
MBS = 256
NBLK = 4
CAP = 8


def draw_cache_k(key, part):
    codes = jax.random.randint(jax.random.fold_in(key, 11), (SECTIONS, TICKS, MBS, KVH, LEN, HD), -127, 128)
    return codes.astype(jnp.float32).astype(jnp.bfloat16)


def draw_cache_v(key, part):
    codes = jax.random.randint(jax.random.fold_in(key, 12), (SECTIONS, TICKS, MBS, KVH, LEN, HD), -127, 128)
    return codes.astype(jnp.float32).astype(jnp.bfloat16)


def draw_k_scale(key, part):
    shape = (SECTIONS, TICKS, MBS, KVH, NBLK)
    base = jnp.exp(jax.random.uniform(jax.random.fold_in(key, 21), shape, jnp.float32, jnp.log(0.004), jnp.log(0.04)))
    return base


def draw_v_scale(key, part):
    shape = (SECTIONS, TICKS, MBS, KVH, NBLK)
    return jnp.exp(jax.random.uniform(jax.random.fold_in(key, 32), shape, jnp.float32, jnp.log(0.004), jnp.log(0.04)))


def steps_of(rng, dims, cuts, low, largest):
    def one(dim, blocks):
        steps = jax.random.uniform(jax.random.fold_in(jax.random.fold_in(rng, 6), dim), (blocks,), jnp.float32, low / len(cuts), largest / len(cuts))
        return jnp.repeat(jnp.exp(steps), dims[dim] // blocks).reshape((-1,) + (1,) * (len(dims) - dim - 1))

    gain = one(*cuts[0])
    for cut in cuts[1:]:
        gain = gain * one(*cut)
    return gain


def length_profile(number_of, total, limit, slope):
    weights = [(1 << 20) // math.isqrt(rank ** slope) + 1 for rank in range(2, number_of + 1)]
    rest, given = total - limit - (number_of - 1), [1] * (number_of - 1)
    while rest > 0:
        movable = [i for i in range(number_of - 1) if given[i] < limit]
        whole, remaining = sum([weights[i] for i in movable]), rest
        for i in movable:
            extra = min(limit - given[i], max(1, remaining * weights[i] // whole), rest)
            given[i] = given[i] + extra
            rest = rest - extra
    return np.array([limit] + given)


def uneven(key, amount, total, limit, slope):
    if amount == 2:
        one = jax.random.randint(key, (), max(1, total - limit), min(limit, total - 1) + 1)
        return jnp.stack([one, total - one])
    tallies = jnp.asarray(length_profile(amount, total, limit, slope), jnp.int32)
    couples = (amount - 1) // 2
    donor, sink = tallies[1:1 + 2 * couples:2], tallies[2:2 + 2 * couples:2]
    margin = jnp.minimum(donor - 1, limit - sink)
    passed = jax.random.randint(jax.random.fold_in(key, 1), (couples,), 0, 1 << 20) % (margin + 1)
    tallies = tallies.at[1:1 + 2 * couples:2].set(donor - passed).at[2:2 + 2 * couples:2].set(sink + passed)
    return tallies[jax.random.permutation(jax.random.fold_in(key, 2), amount)]


def deal_out(key, own, number, rows, number_of, top, bound, skew):
    ranking = jax.random.permutation(key, number_of)
    crowded, ordinary = load_shares(number_of, rows * top, bound, skew, True), load_shares(number_of, rows * top, bound, skew, False)
    places = jnp.arange(number_of)

    def named(sizes, turn):
        used = int((sizes > 0).sum())
        fixed = max(1, used // 4)
        shifted = fixed + (places - fixed + turn * (used - fixed)) % max(1, number_of - fixed)
        return jnp.zeros((number_of,), jnp.int32).at[ranking[jnp.where(places < fixed, places, shifted)]].set(jnp.asarray(sizes, jnp.int32))

    sizes = jnp.where(number % 4 == 0, named(crowded, number // 4), named(ordinary, number - number // 4 - 1))
    mixed = jax.random.permutation(jax.random.fold_in(own, 3), number_of)
    giver, taker = mixed[0:number_of // 2 * 2:2], mixed[1:number_of // 2 * 2:2]
    margin = jnp.minimum(sizes[giver] - 1, bound - sizes[taker]) // 2
    margin = jnp.where((giver == ranking[0]) | (taker == ranking[0]) | (sizes[taker] == 0), 0, jnp.maximum(margin, 0))
    shifted = jax.random.randint(jax.random.fold_in(own, 4), (number_of // 2,), 0, 1 << 20) % (margin + 1)
    sizes = sizes.at[giver].add(-shifted).at[taker].add(shifted)
    items = jnp.searchsorted(jnp.cumsum(sizes), jnp.arange(rows * top), side="right").astype(jnp.int32)
    grid = items.reshape(top, rows).T
    grid = grid[jax.random.permutation(jax.random.fold_in(own, 1), rows)]
    turn = jax.random.randint(jax.random.fold_in(own, 2), (rows, 1), 0, top)
    return jnp.take_along_axis(grid, (jnp.arange(top)[None, :] + turn) % top, axis=1)


def load_shares(number_of, total, bound, skew, full):
    loads = [(1 << 20) // math.isqrt(grade ** skew) + 1 for grade in range(1, number_of + 1)]
    largest = bound if full else min(bound, max(-(-total // number_of), total * loads[0] // sum(loads)))
    least = 1 if total - largest >= number_of - 1 else 0
    holding, spare = [largest] + [least] * (number_of - 1), total - largest - least * (number_of - 1)
    while spare > 0:
        free = [i for i in range(1, number_of) if holding[i] < largest] or [i for i in range(1, number_of) if holding[i] < bound]
        whole, budget = sum([loads[i] for i in free]), spare
        for i in free:
            more = min(bound - holding[i], max(1, budget * loads[i] // whole), spare)
            holding[i] = holding[i] + more
            spare = spare - more
    return np.array(holding)


def scatter_about(key, extent, scale, limit, cuts=(), kind=jnp.bfloat16):
    array = scale * jax.random.normal(key, extent, jnp.float32)
    if cuts:
        array = array * steps_of(key, extent, cuts, -0.22, 0.18)
    return jnp.clip(array, -limit, limit).astype(kind)


def setup_inputs(seed: int = 0) -> dict:
    seeds = jax.random.split(jax.random.key(seed), 19)
    states = scatter_about(seeds[0], (SECTIONS * MBS, D), 1.0, 6.0, ((0, 256),))
    entering = scatter_about(seeds[1], (MBS, D), 1.0, 6.0, ((0, 16),))
    seq_lens = jax.vmap(lambda own: uneven(own, MBS, MBS * LEN // 2, LEN, 2))(jax.random.split(seeds[2], MICRO)).reshape((MICRO, MBS)).astype(jnp.int32)
    routes_keys = jax.random.split(jax.random.fold_in(seeds[3], 1), SECTIONS * TICKS * MBS // TOK_DEV)
    routes_turns = jax.random.permutation(jax.random.fold_in(seeds[3], 3), SECTIONS * TICKS * MBS // TOK_DEV)
    routes = jax.vmap(lambda own, number: deal_out(jax.random.fold_in(seeds[3], 2), own, number, TOK_DEV, EXPERTS, 2, CAP, 0))(routes_keys, routes_turns).reshape((SECTIONS, TICKS, MBS, 2))
    attn_norm = jnp.clip(1.0 + 0.18 * jax.random.normal(seeds[4], (SECTIONS, D), jnp.float32), 0.099609375, 1.8984375).astype(jnp.bfloat16)
    ffn_norm = jnp.clip(1.0 + 0.18 * jax.random.normal(seeds[5], (SECTIONS, D), jnp.float32), 0.099609375, 1.8984375).astype(jnp.bfloat16)
    wq = scatter_about(seeds[6], (SECTIONS, D, QH * HD), D ** -0.5, 0.109375, ((0, 16), (2, 16)))
    wk = scatter_about(seeds[7], (SECTIONS, D, KVH * HD), D ** -0.5, 0.109375, ((0, 16), (2, 16)))
    wv = scatter_about(seeds[8], (SECTIONS, D, KVH * HD), D ** -0.5, 0.109375, ((0, 16), (2, 16)))
    wo = scatter_about(seeds[9], (SECTIONS, QH * HD, D), (QH * HD) ** -0.5, 0.09375, ((0, 16), (1, 16)))
    router = scatter_about(seeds[10], (SECTIONS, D, EXPERTS), (D // 4) ** -0.5, 0.21875, ((0, 16),))
    w_gate = scatter_about(seeds[11], (SECTIONS, D, EXP_WIN * FFE), D ** -0.5, 0.109375, ((0, 16), (2, 16)))
    w_up = scatter_about(seeds[12], (SECTIONS, D, EXP_WIN * FFE), D ** -0.5, 0.109375, ((0, 16), (2, 16)))
    w_down = scatter_about(seeds[13], (SECTIONS, EXP_WIN * FFE, D), (FFE // 4) ** -0.5, 0.125, ((0, 16), (1, 16)))
    cache_k = draw_cache_k(jax.random.fold_in(seeds[18], 71), 0)
    cache_v = draw_cache_v(jax.random.fold_in(seeds[18], 71), 0)
    k_scale = draw_k_scale(jax.random.fold_in(seeds[18], 71), 0)
    v_scale = draw_v_scale(jax.random.fold_in(seeds[18], 71), 0)
    return {"states": states, "entering": entering, "seq_lens": seq_lens, "routes": routes, "attn_norm": attn_norm, "ffn_norm": ffn_norm, "wq": wq, "wk": wk, "wv": wv, "wo": wo, "router": router, "w_gate": w_gate, "w_up": w_up, "w_down": w_down, "cache_k": cache_k, "cache_v": cache_v, "k_scale": k_scale, "v_scale": v_scale}


rope_base = 1000000.0
norm_eps = 1e-05

def rms_scale(values, gain_vec):
    wide = values.astype(jnp.float32)
    factor = lax.rsqrt(lax.optimization_barrier(jnp.mean(wide * wide, axis=-1, keepdims=True)) + norm_eps)
    return (wide * factor * gain_vec.astype(jnp.float32)).astype(jnp.bfloat16)

def rotate(head_vals, lengths_now):
    half_dim = head_vals.shape[-1] // 2
    inv_freq = rope_base ** (-jnp.arange(half_dim, dtype=jnp.float32) * 2.0 / head_vals.shape[-1])
    angles = lengths_now.astype(jnp.float32)[:, None, None] * inv_freq[None, None, :]
    cosine_vals = jnp.cos(angles)
    sine_table = jnp.sin(angles)
    wide = head_vals.astype(jnp.float32)
    lower_half = wide[..., :half_dim]
    upper_half = wide[..., half_dim:]
    turned = jnp.concatenate([lower_half * cosine_vals - upper_half * sine_table, upper_half * cosine_vals + lower_half * sine_table], axis=-1)
    return turned.astype(jnp.bfloat16)

def layer(layer_in, lengths_now, chosen, attn_gain, ffn_gain, wq, wk, wv, wo, router, w_gate, w_up, w_down, key_codes, value_codes, key_scale, value_scale):
    row_count = layer_in.shape[0]
    group_size = QH // KVH
    inverse_square_root = HD ** (-0.5)
    normed = rms_scale(layer_in, attn_gain)
    query_rows = jnp.dot(normed, wq, preferred_element_type=jnp.float32).astype(jnp.bfloat16)
    fresh_key_rows = jnp.dot(normed, wk, preferred_element_type=jnp.float32).astype(jnp.bfloat16)
    value_new = jnp.dot(normed, wv, preferred_element_type=jnp.float32).astype(jnp.bfloat16)
    query_rows = rotate(query_rows.reshape(row_count, QH, HD), lengths_now).reshape(row_count, KVH, group_size, HD)
    fresh_key_rows = rotate(fresh_key_rows.reshape(row_count, KVH, HD), lengths_now)
    value_new = value_new.reshape(row_count, KVH, HD)
    raw_scores = jnp.einsum('bkgd,bkpd->bkgp', query_rows.astype(jnp.float32), key_codes.astype(jnp.float32))
    key_scales = jnp.repeat(key_scale, BLK, axis=-1)
    value_scales = jnp.repeat(value_scale, BLK, axis=-1)
    scores = raw_scores * key_scales[:, :, None, :] * inverse_square_root
    visible = (jnp.arange(LEN, dtype=jnp.int32)[None, :] < lengths_now[:, None])[:, None, None, :]
    current_token_score = jnp.einsum('rwqs,rws->rwq', query_rows.astype(jnp.float32), fresh_key_rows.astype(jnp.float32)) * inverse_square_root
    row_top = jnp.maximum(lax.optimization_barrier(jnp.max(jnp.where(visible, scores, -1e+30), axis=-1)), current_token_score)
    exponent = jnp.where(visible, jnp.exp(scores - row_top[..., None]), 0.0)
    self_weight = jnp.exp(current_token_score - row_top)
    denom_sum = lax.optimization_barrier(jnp.sum(exponent, axis=-1)) + self_weight
    weights = (exponent * value_scales[:, :, None, :]).astype(jnp.bfloat16)
    mixture = jnp.einsum('bkgp,bkpd->bkgd', weights.astype(jnp.float32), value_codes.astype(jnp.float32))
    mixture = mixture + self_weight[..., None] * value_new.astype(jnp.float32)[:, :, None, :]
    attended = (mixture / denom_sum[..., None]).astype(jnp.bfloat16).reshape(row_count, QH * HD)
    residual = (layer_in.astype(jnp.float32) + jnp.dot(attended, wo, preferred_element_type=jnp.float32)).astype(jnp.bfloat16)
    ffn_input = rms_scale(residual, ffn_gain)
    logits = jnp.dot(ffn_input, router, preferred_element_type=jnp.float32)
    picked = jnp.take_along_axis(logits, chosen, axis=1)
    gate_probs = jax.nn.softmax(picked, axis=-1)
    expert_sum = jnp.zeros((row_count, D), jnp.float32)
    for expert_id in range(EXP_WIN):
        gate_act = jnp.dot(ffn_input, w_gate[:, expert_id * FFE:(expert_id + 1) * FFE], preferred_element_type=jnp.float32)
        up_act = jnp.dot(ffn_input, w_up[:, expert_id * FFE:(expert_id + 1) * FFE], preferred_element_type=jnp.float32)
        hidden = (jax.nn.silu(gate_act) * up_act).astype(jnp.bfloat16)
        expert_out = jnp.dot(hidden, w_down[expert_id * FFE:(expert_id + 1) * FFE], preferred_element_type=jnp.float32)
        share = lax.optimization_barrier(jnp.sum(jnp.where(chosen == expert_id, gate_probs, 0.0), axis=-1))
        expert_sum = expert_sum + share[:, None] * expert_out
    return (residual.astype(jnp.float32) + expert_sum).astype(jnp.bfloat16)

def reference(states, entering, seq_lens, routes, attn_norm, ffn_norm, wq, wk, wv, wo, router, w_gate, w_up, w_down, cache_k, cache_v, k_scale, v_scale):

    def run_layer(section_id, tick_index, layer_in):
        return layer(layer_in, seq_lens[section_id + 1 - tick_index], routes[section_id, tick_index], attn_norm[section_id], ffn_norm[section_id], wq[section_id], wk[section_id], wv[section_id], wo[section_id], router[section_id], w_gate[section_id], w_up[section_id], w_down[section_id], cache_k[section_id, tick_index], cache_v[section_id, tick_index], k_scale[section_id, tick_index], v_scale[section_id, tick_index])
    first_tick = [run_layer(section_id, 0, states[section_id * MBS:(section_id + 1) * MBS]) for section_id in range(SECTIONS - 1)]
    second_tick = [run_layer(0, 1, entering)]
    for section_id in range(1, SECTIONS):
        second_tick.append(run_layer(section_id, 1, first_tick[section_id - 1]))
    return jnp.concatenate(second_tick, axis=0)
```

```python
import functools

import jax
import jax.numpy as jnp
from jax import lax
from jax.experimental import pallas as pl
from jax.experimental.pallas import tpu as pltpu
from jax.sharding import PartitionSpec as P

D = 3072
QH = 32
KVH = 8
HD = 128
EXPERTS = 8
EXP_WIN = 1
LEN = 16
BLK = 4
CAP = 8
EP = 16
TOK = 16
CHUNK = 512

rope_base = 1000000.0
norm_eps = 1e-05
f32 = jnp.float32
bf16 = jnp.bfloat16


def call(body, out_shape, n_in, smem=(), name=None, scratch=()):
    specs = [
        pl.BlockSpec(memory_space=pltpu.SMEM if i in smem else pltpu.VMEM) for i in range(n_in)
    ]
    outs = jax.tree.map(lambda _: pl.BlockSpec(memory_space=pltpu.VMEM), out_shape)
    return pl.pallas_call(
        body,
        out_shape=out_shape,
        in_specs=specs,
        out_specs=outs,
        scratch_shapes=list(scratch),
        compiler_params=pltpu.CompilerParams(vmem_limit_bytes=48 << 20),
        name=name,
    )


def columns():
    return [slice(c, c + CHUNK) for c in range(0, D, CHUNK)]


def spread_normed(x_ref, gain_ref, copies_ref):
    total = jnp.zeros((TOK, 1), f32)
    for cols in columns():
        wide = x_ref[:, cols].astype(f32)
        total = total + jnp.sum(wide * wide, axis=-1, keepdims=True)
    factor = lax.rsqrt(total / D + norm_eps)
    for cols in columns():
        wide = x_ref[:, cols].astype(f32)
        rows = (wide * factor * gain_ref[:, cols].astype(f32)).astype(bf16)
        for dest in range(EP):
            copies_ref[dest, :, cols] = rows


def norm_body(x_ref, gain_ref, copies_ref):
    spread_normed(x_ref, gain_ref, copies_ref)


def norm_select_body(first_ref, entering_ref, shifted_ref, gain_ref, x_ref, copies_ref):
    is_first = first_ref[0] == 1

    @pl.when(is_first)
    def _():
        x_ref[...] = entering_ref[...]

    @pl.when(jnp.logical_not(is_first))
    def _():
        x_ref[...] = shifted_ref[...]

    spread_normed(x_ref, gain_ref, copies_ref)


def project_body(x_ref, wq_ref, wk_ref, wv_ref, out_ref):
    x = x_ref[...]
    out_ref[:, 0:256] = jnp.dot(x, wq_ref[...], preferred_element_type=f32).astype(bf16)
    key = jnp.dot(x, wk_ref[...], preferred_element_type=f32)
    value = jnp.dot(x, wv_ref[...], preferred_element_type=f32)
    out_ref[:, 256:384] = jnp.concatenate([key, value], axis=-1).astype(bf16)


def attention_body(
    tick, got_ref, lens_ref, cos_ref, sin_ref, ks_ref, vs_ref, key_ref, value_ref, out_ref
):
    scale = HD ** (-0.5)
    group = QH // KVH
    pos = TOK * LEN
    lane = lax.broadcasted_iota(jnp.int32, (TOK, HD), 1)
    low = lane < HD // 2
    cos_vals = cos_ref[...]
    sin_vals = sin_ref[...]

    def turned(rows):
        return (rows * cos_vals + pltpu.roll(rows, HD // 2, 1) * sin_vals).astype(bf16)

    blocks = KVH * LEN // BLK
    which = lax.broadcasted_iota(jnp.int32, (blocks, KVH * pos), 0)
    at = lax.broadcasted_iota(jnp.int32, (blocks, KVH * pos), 1)
    per_head = LEN // BLK
    spread = jnp.where(
        (which // per_head == at // pos) & (which % per_head == (at % LEN) // BLK), 1.0, 0.0
    ).astype(f32)
    k_all = jnp.dot(
        ks_ref[...], spread, preferred_element_type=f32, precision=lax.Precision.HIGHEST
    )
    v_all = jnp.dot(
        vs_ref[...], spread, preferred_element_type=f32, precision=lax.Precision.HIGHEST
    )
    row = lax.broadcasted_iota(jnp.int32, (TOK, pos), 0)
    col = lax.broadcasted_iota(jnp.int32, (TOK, pos), 1)
    live_one = (col // LEN == row) & (col % LEN < lens_ref[...][:, 0:1])
    live = jnp.concatenate([live_one.astype(f32)] * group, axis=0) > 0.5
    for g in range(KVH):
        first = got_ref[2 * g, :, 256:384].astype(f32)
        second = got_ref[2 * g + 1, :, 256:384].astype(f32)
        key_new = turned(jnp.where(low, first, pltpu.roll(second, HD // 2, 1))).astype(f32)
        value_new = jnp.where(low, pltpu.roll(first, HD // 2, 1), second)
        q = jnp.concatenate(
            [
                turned(got_ref[2 * g + r // 2, :, (r % 2) * HD : (r % 2 + 1) * HD].astype(f32))
                for r in range(group)
            ],
            axis=0,
        )
        keys = key_ref[0, tick, :, g].reshape(pos, HD)
        values = value_ref[0, tick, :, g].reshape(pos, HD)
        k_scale = jnp.concatenate([k_all[:, g * pos : (g + 1) * pos]] * group, axis=0)
        v_scale = jnp.concatenate([v_all[:, g * pos : (g + 1) * pos]] * group, axis=0)
        raw = lax.dot_general(q, keys, (((1,), (1,)), ((), ())), preferred_element_type=f32)
        scores = raw * k_scale * scale
        own = (
            jnp.sum(
                q.astype(f32) * jnp.concatenate([key_new] * group, axis=0), axis=-1, keepdims=True
            )
            * scale
        )
        top = jnp.maximum(jnp.max(jnp.where(live, scores, -1e30), axis=-1, keepdims=True), own)
        e = jnp.where(live, jnp.exp(jnp.where(live, scores, -1e30) - top), 0.0)
        e_own = jnp.exp(own - top)
        denom = jnp.sum(e, axis=-1, keepdims=True) + e_own
        weight = jnp.where(live, e * v_scale, 0.0).astype(bf16)
        mixed = jnp.dot(weight, values, preferred_element_type=f32)
        mixed = mixed + e_own * jnp.concatenate([value_new] * group, axis=0)
        done = (mixed / denom).astype(bf16)
        for r in range(group):
            out_ref[2 * g + r // 2, :, (r % 2) * HD : (r % 2 + 1) * HD] = done[
                r * TOK : (r + 1) * TOK
            ]


def out_body(att_ref, wo_ref, part_ref):
    part_ref[...] = jnp.dot(att_ref[...], wo_ref[0], preferred_element_type=f32).astype(bf16)


def residual_body(
    x_ref, got_ref, gain_ref, router_ref, chosen_ref, sel_ref, sel_t_ref, res_ref, copies_ref, coef_ref, ffn_ref
):
    total = jnp.zeros((TOK, 1), f32)
    for cols in columns():
        acc = got_ref[0, :, cols].astype(f32)
        for src in range(1, EP):
            acc = acc + got_ref[src, :, cols].astype(f32)
        rounded = (x_ref[:, cols].astype(f32) + acc).astype(bf16)
        res_ref[:, cols] = rounded
        wide = rounded.astype(f32)
        total = total + jnp.sum(wide * wide, axis=-1, keepdims=True)
    factor = lax.rsqrt(total / D + norm_eps)
    for cols in columns():
        wide = res_ref[:, cols].astype(f32)
        rows = (wide * factor * gain_ref[:, cols].astype(f32)).astype(bf16)
        ffn_ref[:, cols] = rows
        slots = jnp.dot(sel_ref[...], rows, preferred_element_type=f32).astype(bf16)
        for dest in range(EP):
            copies_ref[dest, :, cols] = slots
    logits = jnp.dot(ffn_ref[...], router_ref[0], preferred_element_type=f32)
    expert = lax.broadcasted_iota(jnp.int32, (TOK, EXPERTS), 1)
    one = chosen_ref[:, 0:1]
    two = chosen_ref[:, 1:2]
    pick_one = jnp.sum(jnp.where(expert == one, logits, 0.0), axis=-1, keepdims=True)
    pick_two = jnp.sum(jnp.where(expert == two, logits, 0.0), axis=-1, keepdims=True)
    top = jnp.maximum(pick_one, pick_two)
    e_one = jnp.exp(pick_one - top)
    e_two = jnp.exp(pick_two - top)
    both = e_one + e_two
    share = jnp.where(one == 0, e_one / both, 0.0) + jnp.where(two == 0, e_two / both, 0.0)
    coef_ref[...] = share * sel_t_ref[...]


def expert_body(x_ref, gate_ref, up_ref, down_ref, part_ref):
    x = x_ref[...]
    gate = jnp.dot(x, gate_ref[0], preferred_element_type=f32)
    up = jnp.dot(x, up_ref[0], preferred_element_type=f32)
    hidden = (gate * jax.nn.sigmoid(gate) * up).astype(bf16)
    part_ref[...] = jnp.dot(hidden, down_ref[0], preferred_element_type=f32).astype(bf16)


def combine_body(res_ref, coef_ref, got_ref, out_ref):
    coef = coef_ref[...]
    for cols in columns():
        acc = got_ref[0, :, cols].astype(f32)
        for src in range(1, EP):
            acc = acc + got_ref[src, :, cols].astype(f32)
        total = res_ref[:, cols].astype(f32)
        for k in range(CAP):
            total = total + coef[:, k : k + 1] * acc[k : k + 1, :]
        out_ref[:, cols] = total.astype(bf16)


def sds(shape, dtype):
    return jax.ShapeDtypeStruct(shape, dtype)


def trade(pieces):
    return lax.all_to_all(pieces, "ep", split_axis=0, concat_axis=0, tiled=True)


def local(
    states,
    entering,
    seq_lens,
    routes,
    attn_norm,
    ffn_norm,
    wq,
    wk,
    wv,
    wo,
    router,
    w_gate,
    w_up,
    w_down,
    cache_k,
    cache_v,
    k_scale,
    v_scale,
):
    ep_index = lax.axis_index("ep")
    section_index = lax.axis_index("section")
    lens = lax.dynamic_slice(seq_lens, (section_index, ep_index * TOK), (2, TOK))[::-1]
    half = HD // 2
    inv_freq = rope_base ** (-jnp.arange(half, dtype=f32) * 2.0 / HD)
    angles = lens.astype(f32)[:, :, None] * inv_freq
    cos_vals = jnp.cos(angles)
    sin_vals = jnp.sin(angles)
    cos_vals = jnp.concatenate([cos_vals, cos_vals], axis=-1)
    sin_vals = jnp.concatenate([-sin_vals, sin_vals], axis=-1)
    lens_rows = jnp.broadcast_to(lens[:, :, None], (2, TOK, HD))
    ks = k_scale[0].reshape(2, TOK, KVH * LEN // BLK)
    vs = v_scale[0].reshape(2, TOK, KVH * LEN // BLK)
    held = jnp.any(routes[0] == 0, axis=-1)
    before = jnp.arange(TOK)[:, None] > jnp.arange(TOK)[None, :]
    rank = jnp.sum(jnp.where(before & held[:, None, :], 1, 0), axis=-1)
    slot = jnp.arange(CAP, dtype=jnp.int32)
    sel = (held[:, None, :] & (rank[:, None, :] == slot[:, None])).astype(bf16)
    sel_t = (held[:, :, None] & (rank[:, :, None] == slot)).astype(f32)
    sel_t = jnp.pad(sel_t, ((0, 0), (0, 0), (0, HD - CAP)))

    def run_layer(x, copies, tick):
        everyone = trade(copies).reshape(EP * TOK, D)
        projected = call(project_body, sds((EP * TOK, 384), bf16), 4, name="project")(
            everyone, wq[0], wk[0], wv[0]
        )
        got = trade(projected.reshape(EP, TOK, 384))
        attended = call(
            functools.partial(attention_body, tick), sds((EP, TOK, 256), bf16), 8, name="attend"
        )(got, lens_rows[tick], cos_vals[tick], sin_vals[tick], ks[tick], vs[tick], cache_k, cache_v)
        heads = trade(attended).reshape(EP * TOK, 256)
        part = call(out_body, sds((EP * TOK, D), bf16), 2, name="outproj")(heads, wo)
        sums = trade(part.reshape(EP, TOK, D))
        residual, slots, coef = call(
            residual_body,
            (sds((TOK, D), bf16), sds((EP, CAP, D), bf16), sds((TOK, HD), f32)),
            7,
            name="residual",
            scratch=[pltpu.VMEM((TOK, D), bf16)],
        )(x, sums, ffn_norm, router, routes[0, tick], sel[tick], sel_t[tick])
        landed = trade(slots).reshape(EP * CAP, D)
        pieces = call(expert_body, sds((EP * CAP, D), bf16), 4, name="expert")(
            landed, w_gate, w_up, w_down
        )
        returned = trade(pieces.reshape(EP, CAP, D))
        return call(combine_body, sds((TOK, D), bf16), 3, name="combine")(
            residual, coef, returned
        )

    copies = call(norm_body, sds((EP, TOK, D), bf16), 2, name="norm")(states, attn_norm)
    first_out = run_layer(states, copies, 0)
    count = lax.axis_size("section")
    shifted = lax.ppermute(first_out, "section", [(i, i + 1) for i in range(count - 1)])
    is_first = (section_index == 0).astype(jnp.int32).reshape(1)
    second_in, copies = call(
        norm_select_body,
        (sds((TOK, D), bf16), sds((EP, TOK, D), bf16)),
        4,
        smem=(0,),
        name="select_norm",
    )(is_first, entering, shifted, attn_norm)
    return run_layer(second_in, copies, 1)


def solution(mesh):
    return jax.shard_map(
        local,
        mesh=mesh,
        in_specs=(
            P(("section", "ep"), None),
            P("ep", None),
            P(),
            P("section", None, "ep", None),
            P("section", None),
            P("section", None),
            P("section", None, "ep"),
            P("section", None, "ep"),
            P("section", None, "ep"),
            P("section", "ep", None),
            P("section", None, None),
            P("section", None, "ep"),
            P("section", None, "ep"),
            P("section", "ep", None),
            P("section", None, "ep", None, None, None),
            P("section", None, "ep", None, None, None),
            P("section", None, "ep", None, None),
            P("section", None, "ep", None, None),
        ),
        out_specs=P(("section", "ep"), None),
        check_vma=False,
    )
```

```python
import functools

import jax
import jax.numpy as jnp
import numpy as np
from jax import lax
from jax.experimental import pallas as pl
from jax.experimental.pallas import tpu as pltpu
from jax.sharding import PartitionSpec as P

D = 3072
QH = 32
KVH = 8
HD = 128
EXPERTS = 8
EXP_WIN = 1
LEN = 16
BLK = 4
CAP = 8
EP = 16
TOK = 16
CHUNK = 512

rope_base = 1000000.0
norm_eps = 1e-05
f32 = jnp.float32
bf16 = jnp.bfloat16


def call(body, out_shape, n_in, smem=(), name=None, scratch=(), limit=12, space=pltpu.VMEM):
    specs = [pl.BlockSpec(memory_space=pltpu.SMEM if i in smem else space) for i in range(n_in)]
    outs = jax.tree.map(lambda _: pl.BlockSpec(memory_space=pltpu.VMEM), out_shape)
    return pl.pallas_call(
        body,
        out_shape=out_shape,
        in_specs=specs,
        out_specs=outs,
        scratch_shapes=list(scratch),
        compiler_params=pltpu.CompilerParams(vmem_limit_bytes=limit << 20),
        name=name,
    )


def dot_last(left, right):
    return lax.dot_general(left, right, (((1,), (1,)), ((), ())), preferred_element_type=f32)


def dot_first(left, right):
    return lax.dot_general(
        left,
        right,
        (((0,), (0,)), ((), ())),
        preferred_element_type=f32,
        precision=lax.Precision.HIGHEST,
    )


def columns():
    return [slice(c, c + CHUNK) for c in range(0, D, CHUNK)]


def spread_normed(x_ref, gain_ref, copies_ref):
    total = jnp.zeros((TOK, 1), f32)
    for cols in columns():
        wide = x_ref[:, cols].astype(f32)
        total = total + jnp.sum(wide * wide, axis=-1, keepdims=True)
    factor = lax.rsqrt(total / D + norm_eps)
    for cols in columns():
        wide = x_ref[:, cols].astype(f32)
        rows = (wide * factor * gain_ref[:, cols].astype(f32)).astype(bf16)
        for dest in range(EP):
            copies_ref[dest, :, cols] = rows


def norm_body(x_hbm, gain_hbm, copies_ref, x_ref, gain_ref, sems):
    fetches = [
        pltpu.make_async_copy(x_hbm, x_ref, sems.at[0]),
        pltpu.make_async_copy(gain_hbm, gain_ref, sems.at[1]),
    ]
    for fetch in fetches:
        fetch.start()
    for fetch in fetches:
        fetch.wait()
    spread_normed(x_ref, gain_ref, copies_ref)


def norm_select_body(entering_ref, shifted_ref, gain_ref, x_ref, copies_ref):
    is_first = lax.axis_index("section") == 0

    @pl.when(is_first)
    def _():
        x_ref[...] = entering_ref[...]

    @pl.when(jnp.logical_not(is_first))
    def _():
        x_ref[...] = shifted_ref[...]

    spread_normed(x_ref, gain_ref, copies_ref)


def project_body(x_ref, wq_ref, wk_ref, wv_ref, out_ref):
    x = x_ref[...]
    out_ref[:, 0:256] = jnp.dot(x, wq_ref[...], preferred_element_type=f32).astype(bf16)
    both = jnp.concatenate([wk_ref[...], wv_ref[...]], axis=0)
    out_ref[:, 256:384] = dot_last(x, both).astype(bf16)


def rotary_table():
    half = HD // 2
    inv_freq = rope_base ** (-np.arange(half, dtype=np.float64) * 2.0 / HD)
    angles = np.arange(2 * LEN, dtype=np.float64)[:, None] * inv_freq
    cos_vals, sin_vals = np.cos(angles), np.sin(angles)
    return np.concatenate([cos_vals, cos_vals, -sin_vals, sin_vals], axis=1).astype(np.float32)


def attention_body(
    tick, got_ref, lens_ref, rotary_ref, ks_ref, vs_ref, key_ref, value_ref, out_ref
):
    scale = HD ** (-0.5)
    group = QH // KVH
    pos = TOK * LEN
    lane = lax.broadcasted_iota(jnp.int32, (TOK, HD), 1)
    low = lane < HD // 2
    row_lens = lens_ref[pl.ds(lax.axis_index("section") + 1 - tick, 1), :].astype(f32)
    mine = lax.broadcasted_iota(jnp.int32, (TOK, row_lens.shape[1]), 0) + lax.axis_index("ep") * TOK
    there = lax.broadcasted_iota(jnp.int32, (TOK, row_lens.shape[1]), 1)
    lens = jnp.sum(jnp.where(mine == there, row_lens, 0.0), axis=-1, keepdims=True)
    lens = lens.astype(jnp.int32)
    length = lax.broadcasted_iota(jnp.int32, (TOK, 2 * LEN), 1)
    rotary = jnp.dot(
        jnp.where(length == lens, 1.0, 0.0).astype(f32),
        rotary_ref[...],
        preferred_element_type=f32,
        precision=lax.Precision.HIGHEST,
    )
    cos_vals = rotary[:, 0:HD]
    sin_vals = rotary[:, HD : 2 * HD]

    def turned(rows):
        return (rows * cos_vals + pltpu.roll(rows, HD // 2, 1) * sin_vals).astype(bf16)

    blocks = LEN // BLK
    which = lax.broadcasted_iota(jnp.int32, (KVH * blocks, KVH * pos), 0)
    at = lax.broadcasted_iota(jnp.int32, (KVH * blocks, KVH * pos), 1)
    spread = jnp.where(
        (which // blocks == at // pos) & (which % blocks == (at % LEN) // BLK), 1.0, 0.0
    ).astype(f32)
    k_all = dot_first(jnp.concatenate([ks_ref[tick, g] for g in range(KVH)], axis=0), spread)
    v_all = dot_first(jnp.concatenate([vs_ref[tick, g] for g in range(KVH)], axis=0), spread)
    row = lax.broadcasted_iota(jnp.int32, (TOK, pos), 0)
    col = lax.broadcasted_iota(jnp.int32, (TOK, pos), 1)
    live_one = (col // LEN == row) & (col % LEN < lens)
    live = jnp.concatenate([live_one.astype(f32)] * group, axis=0) > 0.5
    for g in range(KVH):
        first = got_ref[2 * g, :, 256:384].astype(f32)
        second = got_ref[2 * g + 1, :, 256:384].astype(f32)
        key_new = turned(jnp.where(low, first, pltpu.roll(second, HD // 2, 1))).astype(f32)
        value_new = jnp.where(low, pltpu.roll(first, HD // 2, 1), second)
        q = jnp.concatenate(
            [
                turned(got_ref[2 * g + r // 2, :, (r % 2) * HD : (r % 2 + 1) * HD].astype(f32))
                for r in range(group)
            ],
            axis=0,
        )
        keys = key_ref[0, tick, :, g].reshape(pos, HD)
        values = value_ref[0, tick, :, g].reshape(pos, HD)
        k_scale = jnp.concatenate([k_all[:, g * pos : (g + 1) * pos]] * group, axis=0)
        v_scale = jnp.concatenate([v_all[:, g * pos : (g + 1) * pos]] * group, axis=0)
        scores = dot_last(q, keys) * k_scale * scale
        own = (
            jnp.sum(
                q.astype(f32) * jnp.concatenate([key_new] * group, axis=0), axis=-1, keepdims=True
            )
            * scale
        )
        top = jnp.maximum(jnp.max(jnp.where(live, scores, -1e30), axis=-1, keepdims=True), own)
        e = jnp.where(live, jnp.exp(jnp.where(live, scores, -1e30) - top), 0.0)
        e_own = jnp.exp(own - top)
        denom = jnp.sum(e, axis=-1, keepdims=True) + e_own
        weight = jnp.where(live, e * v_scale, 0.0).astype(bf16)
        mixed = jnp.dot(weight, values, preferred_element_type=f32)
        mixed = mixed + e_own * jnp.concatenate([value_new] * group, axis=0)
        done = (mixed / denom).astype(bf16)
        for r in range(group):
            out_ref[2 * g + r // 2, :, (r % 2) * HD : (r % 2 + 1) * HD] = done[
                r * TOK : (r + 1) * TOK
            ]


def out_body(att_ref, wo_ref, part_ref):
    part_ref[...] = jnp.dot(att_ref[...], wo_ref[0], preferred_element_type=f32).astype(bf16)


def residual_body(
    tick, x_ref, got_ref, gain_ref, router_ref, chosen_ref, res_ref, copies_ref, coef_ref, ffn_ref
):
    one = chosen_ref[tick, 0:1, :]
    two = chosen_ref[tick, 1:2, :]
    held = jnp.where((one == 0) | (two == 0), 1.0, 0.0).astype(f32)
    held = jnp.broadcast_to(held, (CAP, TOK))
    before = lax.broadcasted_iota(jnp.int32, (TOK, TOK), 0) < lax.broadcasted_iota(
        jnp.int32, (TOK, TOK), 1
    )
    rank = jnp.dot(
        held.astype(bf16), before.astype(f32).astype(bf16), preferred_element_type=f32
    )
    slot = lax.broadcasted_iota(jnp.int32, (CAP, TOK), 0).astype(f32)
    sel = jnp.where((held > 0.5) & (rank == slot), 1.0, 0.0).astype(f32)
    total = jnp.zeros((TOK, 1), f32)
    for cols in columns():
        acc = got_ref[0, :, cols].astype(f32)
        for src in range(1, EP):
            acc = acc + got_ref[src, :, cols].astype(f32)
        rounded = (x_ref[:, cols].astype(f32) + acc).astype(bf16)
        res_ref[:, cols] = rounded
        wide = rounded.astype(f32)
        total = total + jnp.sum(wide * wide, axis=-1, keepdims=True)
    factor = lax.rsqrt(total / D + norm_eps)
    for cols in columns():
        wide = res_ref[:, cols].astype(f32)
        rows = (wide * factor * gain_ref[:, cols].astype(f32)).astype(bf16)
        ffn_ref[:, cols] = rows
        slots = jnp.dot(sel.astype(bf16), rows, preferred_element_type=f32).astype(bf16)
        for dest in range(EP):
            copies_ref[dest, :, cols] = slots
    logits = dot_last(router_ref[...], ffn_ref[...])
    expert = lax.broadcasted_iota(jnp.int32, (EXPERTS, TOK), 0)
    pick_one = jnp.sum(jnp.where(expert == one, logits, 0.0), axis=0, keepdims=True)
    pick_two = jnp.sum(jnp.where(expert == two, logits, 0.0), axis=0, keepdims=True)
    top = jnp.maximum(pick_one, pick_two)
    e_one = jnp.exp(pick_one - top)
    e_two = jnp.exp(pick_two - top)
    both = e_one + e_two
    share = jnp.where(one == 0, e_one / both, 0.0) + jnp.where(two == 0, e_two / both, 0.0)
    coef_ref[...] = share * sel


def expert_body(x_ref, gate_ref, up_ref, down_ref, part_ref):
    x = x_ref[...]
    gate = dot_last(x, gate_ref[...])
    up = dot_last(x, up_ref[...])
    hidden = (gate * jax.nn.sigmoid(gate) * up).astype(bf16)
    part_ref[...] = jnp.dot(hidden, down_ref[0], preferred_element_type=f32).astype(bf16)


def combine_body(res_ref, coef_ref, got_ref, out_ref):
    coef = coef_ref[...]
    for cols in columns():
        acc = got_ref[0, :, cols].astype(f32)
        for src in range(1, EP):
            acc = acc + got_ref[src, :, cols].astype(f32)
        out_ref[:, cols] = (res_ref[:, cols].astype(f32) + dot_first(coef, acc)).astype(bf16)


def sds(shape, dtype):
    return jax.ShapeDtypeStruct(shape, dtype)


def trade(pieces):
    return lax.all_to_all(pieces, "ep", split_axis=0, concat_axis=0, tiled=True)


def local(
    states,
    entering,
    seq_lens,
    routes,
    attn_norm,
    ffn_norm,
    wq,
    wk,
    wv,
    wo,
    router,
    w_gate,
    w_up,
    w_down,
    cache_k,
    cache_v,
    k_scale,
    v_scale,
):
    rotary = rotary_table()
    ks = jnp.transpose(k_scale[0], (0, 2, 3, 1))
    vs = jnp.transpose(v_scale[0], (0, 2, 3, 1))
    chosen = jnp.transpose(routes[0], (0, 2, 1))
    wk_t, wv_t, router_t, gate_t, up_t = (
        jnp.transpose(w[0], (1, 0)) for w in (wk, wv, router, w_gate, w_up)
    )

    def run_layer(x, copies, tick):
        everyone = trade(copies).reshape(EP * TOK, D)
        projected = call(project_body, sds((EP * TOK, 384), bf16), 4, name="project")(
            everyone, wq[0], wk_t, wv_t
        )
        got = trade(projected.reshape(EP, TOK, 384))
        attended = call(
            functools.partial(attention_body, tick),
            sds((EP, TOK, 256), bf16),
            7,
            name="attend",
        )(got, seq_lens, rotary, ks, vs, cache_k, cache_v)
        heads = trade(attended).reshape(EP * TOK, 256)
        part = call(out_body, sds((EP * TOK, D), bf16), 2, name="outproj")(heads, wo)
        sums = trade(part.reshape(EP, TOK, D))
        residual, slots, coef = call(
            functools.partial(residual_body, tick),
            (sds((TOK, D), bf16), sds((EP, CAP, D), bf16), sds((CAP, TOK), f32)),
            5,
            name="residual",
            scratch=[pltpu.VMEM((TOK, D), bf16)],
        )(x, sums, ffn_norm, router_t, chosen)
        landed = trade(slots).reshape(EP * CAP, D)
        pieces = call(expert_body, sds((EP * CAP, D), bf16), 4, name="expert", limit=16)(
            landed, gate_t, up_t, w_down
        )
        returned = trade(pieces.reshape(EP, CAP, D))
        return call(combine_body, sds((TOK, D), bf16), 3, name="combine")(
            residual, coef, returned
        )

    copies = call(
        norm_body,
        sds((EP, TOK, D), bf16),
        2,
        name="norm",
        scratch=[
            pltpu.VMEM((TOK, D), bf16),
            pltpu.VMEM((1, D), bf16),
            pltpu.SemaphoreType.DMA((2,)),
        ],
        space=pltpu.HBM,
    )(states, attn_norm)
    first_out = run_layer(states, copies, 0)
    count = lax.axis_size("section")
    shifted = lax.ppermute(first_out, "section", [(i, i + 1) for i in range(count - 1)])
    second_in, copies = call(
        norm_select_body,
        (sds((TOK, D), bf16), sds((EP, TOK, D), bf16)),
        3,
        name="select_norm",
    )(entering, shifted, attn_norm)
    return run_layer(second_in, copies, 1)


def solution(mesh):
    return jax.shard_map(
        local,
        mesh=mesh,
        in_specs=(
            P(("section", "ep"), None),
            P("ep", None),
            P(),
            P("section", None, "ep", None),
            P("section", None),
            P("section", None),
            P("section", None, "ep"),
            P("section", None, "ep"),
            P("section", None, "ep"),
            P("section", "ep", None),
            P("section", None, None),
            P("section", None, "ep"),
            P("section", None, "ep"),
            P("section", "ep", None),
            P("section", None, "ep", None, None, None),
            P("section", None, "ep", None, None, None),
            P("section", None, "ep", None, None),
            P("section", None, "ep", None, None),
        ),
        out_specs=P(("section", "ep"), None),
        check_vma=False,
    )
```

```python
import functools

import jax
import jax.numpy as jnp
import numpy as np
from jax import lax
from jax.experimental import pallas as pl
from jax.experimental.pallas import tpu as pltpu
from jax.sharding import PartitionSpec as P

D = 3072
QH = 32
KVH = 8
HD = 128
EXPERTS = 8
EXP_WIN = 1
LEN = 16
BLK = 4
CAP = 8
EP = 16
TOK = 16
CHUNK = 512
HALF = D // 2
QKV = 384

rope_base = 1000000.0
norm_eps = 1e-05
f32 = jnp.float32
bf16 = jnp.bfloat16


def call(body, out_shape, n_in, smem=(), name=None, scratch=(), limit=12, space=pltpu.VMEM):
    specs = [pl.BlockSpec(memory_space=pltpu.SMEM if i in smem else space) for i in range(n_in)]
    outs = jax.tree.map(lambda _: pl.BlockSpec(memory_space=pltpu.VMEM), out_shape)
    return pl.pallas_call(
        body,
        out_shape=out_shape,
        in_specs=specs,
        out_specs=outs,
        scratch_shapes=list(scratch),
        compiler_params=pltpu.CompilerParams(vmem_limit_bytes=limit << 20),
        name=name,
    )


def dot_last(left, right):
    return lax.dot_general(left, right, (((1,), (1,)), ((), ())), preferred_element_type=f32)


def dot_first(left, right):
    return lax.dot_general(
        left,
        right,
        (((0,), (0,)), ((), ())),
        preferred_element_type=f32,
        precision=lax.Precision.HIGHEST,
    )


def columns():
    return [slice(c, c + CHUNK) for c in range(0, D, CHUNK)]


def turn_of():
    return lax.axis_index("section") & 1


def x_partner(device, turn):
    x = device & 3
    odd = ((((x + 1) & 3) ^ 1) + 3) & 3
    return (device - x) + jnp.where(turn == 0, x ^ 1, odd)


def y_partner(device, turn):
    y = device >> 2
    odd = ((((y + 1) & 3) ^ 1) + 3) & 3
    return (device & 3) + 4 * jnp.where(turn == 0, y ^ 1, odd)


def partner_list(partner, sections):
    def odd_pair(v):
        return ((((v + 1) & 3) ^ 1) + 3) & 3

    pairs = []
    for section in range(sections):
        for device in range(EP):
            y, x = divmod(device, 4)
            if partner == "x":
                x = x ^ 1 if section % 2 == 0 else odd_pair(x)
            else:
                y = y ^ 1 if section % 2 == 0 else odd_pair(y)
            pairs.append((section * EP + device, section * EP + 4 * y + x))
    return pairs


def spread_normed(x_ref, gain_ref, copies_ref, halves):
    total = jnp.zeros((TOK, 1), f32)
    for cols in columns():
        wide = x_ref[:, cols].astype(f32)
        total = total + jnp.sum(wide * wide, axis=-1, keepdims=True)
    factor = lax.rsqrt(total / D + norm_eps)
    turn = turn_of()
    for cols in columns():
        wide = x_ref[:, cols].astype(f32)
        rows = (wide * factor * gain_ref[:, cols].astype(f32)).astype(bf16)
        if not halves:
            for dest in range(EP):
                copies_ref[dest, :, cols] = rows
        else:
            part = cols.start // HALF
            kept = slice(cols.start - part * HALF, cols.stop - part * HALF)
            for k in range(2):
                for x in range(4):
                    copies_ref[(2 * k + (turn ^ part)) * 4 + x, :, kept] = rows


def norm_body(x_hbm, gain_hbm, copies_ref, x_ref, gain_ref, sems):
    fetches = [
        pltpu.make_async_copy(x_hbm, x_ref, sems.at[0]),
        pltpu.make_async_copy(gain_hbm, gain_ref, sems.at[1]),
    ]
    for fetch in fetches:
        fetch.start()
    for fetch in fetches:
        fetch.wait()
    spread_normed(x_ref, gain_ref, copies_ref, False)


def norm_select_body(entering_ref, shifted_ref, gain_ref, x_ref, copies_ref):
    is_first = lax.axis_index("section") == 0

    @pl.when(is_first)
    def _():
        x_ref[...] = entering_ref[...]

    @pl.when(jnp.logical_not(is_first))
    def _():
        x_ref[...] = shifted_ref[...]

    spread_normed(x_ref, gain_ref, copies_ref, True)


def project_body(x_ref, wq_ref, wk_ref, wv_ref, out_ref):
    x = x_ref[...]
    out_ref[:, 0:256] = jnp.dot(x, wq_ref[...], preferred_element_type=f32).astype(bf16)
    both = jnp.concatenate([wk_ref[...], wv_ref[...]], axis=0)
    out_ref[:, 256:384] = dot_last(x, both).astype(bf16)


def project_halves_body(x_ref, wq_ref, wk_ref, wv_ref, q_ref, kv_ref, out_ref):
    x = x_ref[...]
    at = pl.multiple_of(((lax.axis_index("ep") >> 2) + turn_of()) % 2 * HALF, HALF)
    own_q = wq_ref[pl.ds(at, HALF), :]
    own_kv = jnp.concatenate([wk_ref[:, pl.ds(at, HALF)], wv_ref[:, pl.ds(at, HALF)]], axis=0)
    out_ref[:, 0:256] = jnp.dot(x, own_q, preferred_element_type=f32).astype(bf16)
    out_ref[:, 256:QKV] = dot_last(x, own_kv).astype(bf16)
    out_ref[:, QKV : QKV + 256] = jnp.dot(x, q_ref[...], preferred_element_type=f32).astype(bf16)
    out_ref[:, QKV + 256 : 2 * QKV] = dot_last(x, kv_ref[...]).astype(bf16)


def rotary_table():
    half = HD // 2
    inv_freq = rope_base ** (-np.arange(half, dtype=np.float64) * 2.0 / HD)
    angles = np.arange(2 * LEN, dtype=np.float64)[:, None] * inv_freq
    cos_vals, sin_vals = np.cos(angles), np.sin(angles)
    return np.concatenate([cos_vals, cos_vals, -sin_vals, sin_vals], axis=1).astype(np.float32)


def attention_body(
    tick, got_ref, lens_ref, rotary_ref, ks_ref, vs_ref, key_ref, value_ref, out_ref
):
    scale = HD ** (-0.5)
    group = QH // KVH
    pos = TOK * LEN
    lane = lax.broadcasted_iota(jnp.int32, (TOK, HD), 1)
    low = lane < HD // 2
    turn = turn_of()

    def rows_of(src, start, stop):
        rows = got_ref[src, :, start:stop].astype(f32)
        if tick == 1:
            other = got_ref[y_partner(src, turn), :, QKV + start : QKV + stop].astype(f32)
            rows = (rows + other).astype(bf16).astype(f32)
        return rows

    row_lens = lens_ref[pl.ds(lax.axis_index("section") + 1 - tick, 1), :].astype(f32)
    mine = lax.broadcasted_iota(jnp.int32, (TOK, row_lens.shape[1]), 0) + lax.axis_index("ep") * TOK
    there = lax.broadcasted_iota(jnp.int32, (TOK, row_lens.shape[1]), 1)
    lens = jnp.sum(jnp.where(mine == there, row_lens, 0.0), axis=-1, keepdims=True)
    lens = lens.astype(jnp.int32)
    length = lax.broadcasted_iota(jnp.int32, (TOK, 2 * LEN), 1)
    rotary = jnp.dot(
        jnp.where(length == lens, 1.0, 0.0).astype(f32),
        rotary_ref[...],
        preferred_element_type=f32,
        precision=lax.Precision.HIGHEST,
    )
    cos_vals = rotary[:, 0:HD]
    sin_vals = rotary[:, HD : 2 * HD]

    def turned(rows):
        return (rows * cos_vals + pltpu.roll(rows, HD // 2, 1) * sin_vals).astype(bf16)

    blocks = LEN // BLK
    which = lax.broadcasted_iota(jnp.int32, (KVH * blocks, KVH * pos), 0)
    at = lax.broadcasted_iota(jnp.int32, (KVH * blocks, KVH * pos), 1)
    spread = jnp.where(
        (which // blocks == at // pos) & (which % blocks == (at % LEN) // BLK), 1.0, 0.0
    ).astype(f32)
    k_all = dot_first(jnp.concatenate([ks_ref[tick, g] for g in range(KVH)], axis=0), spread)
    v_all = dot_first(jnp.concatenate([vs_ref[tick, g] for g in range(KVH)], axis=0), spread)
    row = lax.broadcasted_iota(jnp.int32, (TOK, pos), 0)
    col = lax.broadcasted_iota(jnp.int32, (TOK, pos), 1)
    live_one = (col // LEN == row) & (col % LEN < lens)
    live = jnp.concatenate([live_one.astype(f32)] * group, axis=0) > 0.5
    for g in range(KVH):
        first = rows_of(2 * g, 256, QKV)
        second = rows_of(2 * g + 1, 256, QKV)
        key_new = turned(jnp.where(low, first, pltpu.roll(second, HD // 2, 1))).astype(f32)
        value_new = jnp.where(low, pltpu.roll(first, HD // 2, 1), second)
        q = jnp.concatenate(
            [
                turned(rows_of(2 * g + r // 2, (r % 2) * HD, (r % 2 + 1) * HD))
                for r in range(group)
            ],
            axis=0,
        )
        keys = key_ref[0, tick, :, g].reshape(pos, HD)
        values = value_ref[0, tick, :, g].reshape(pos, HD)
        k_scale = jnp.concatenate([k_all[:, g * pos : (g + 1) * pos]] * group, axis=0)
        v_scale = jnp.concatenate([v_all[:, g * pos : (g + 1) * pos]] * group, axis=0)
        scores = dot_last(q, keys) * k_scale * scale
        own = (
            jnp.sum(
                q.astype(f32) * jnp.concatenate([key_new] * group, axis=0), axis=-1, keepdims=True
            )
            * scale
        )
        top = jnp.maximum(jnp.max(jnp.where(live, scores, -1e30), axis=-1, keepdims=True), own)
        e = jnp.where(live, jnp.exp(jnp.where(live, scores, -1e30) - top), 0.0)
        e_own = jnp.exp(own - top)
        denom = jnp.sum(e, axis=-1, keepdims=True) + e_own
        weight = jnp.where(live, e * v_scale, 0.0).astype(bf16)
        mixed = jnp.dot(weight, values, preferred_element_type=f32)
        mixed = mixed + e_own * jnp.concatenate([value_new] * group, axis=0)
        done = (mixed / denom).astype(bf16)
        for r in range(group):
            rows = done[r * TOK : (r + 1) * TOK]
            at = (r % 2) * HD
            owner = 2 * g + r // 2
            out_ref[owner, :, at : at + HD] = rows
            out_ref[x_partner(owner, turn), :, 256 + at : 256 + at + HD] = rows


def out_body(att_ref, wo_ref, other_ref, part_ref):
    at = pl.multiple_of((lax.axis_index("ep") + turn_of()) % 2 * HALF, HALF)
    own = wo_ref[0, :, pl.ds(at, HALF)]
    total = jnp.dot(att_ref[:, 0:256], own, preferred_element_type=f32)
    total = total + jnp.dot(att_ref[:, 256:512], other_ref[...], preferred_element_type=f32)
    part_ref[...] = total.astype(bf16)


def residual_body(
    tick, x_ref, got_ref, gain_ref, router_ref, chosen_ref, res_ref, copies_ref, coef_ref, ffn_ref
):
    one = chosen_ref[tick, 0:1, :]
    two = chosen_ref[tick, 1:2, :]
    held = jnp.where((one == 0) | (two == 0), 1.0, 0.0).astype(f32)
    held = jnp.broadcast_to(held, (CAP, TOK))
    before = lax.broadcasted_iota(jnp.int32, (TOK, TOK), 0) < lax.broadcasted_iota(
        jnp.int32, (TOK, TOK), 1
    )
    rank = jnp.dot(
        held.astype(bf16), before.astype(f32).astype(bf16), preferred_element_type=f32
    )
    slot = lax.broadcasted_iota(jnp.int32, (CAP, TOK), 0).astype(f32)
    sel = jnp.where((held > 0.5) & (rank == slot), 1.0, 0.0).astype(f32)
    total = jnp.zeros((TOK, 1), f32)
    for cols in columns():
        part = cols.start // HALF
        held_cols = slice(cols.start - part * HALF, cols.stop - part * HALF)
        first = turn_of() ^ part
        acc = got_ref[first, :, held_cols].astype(f32)
        for pair in range(1, EP // 2):
            acc = acc + got_ref[2 * pair + first, :, held_cols].astype(f32)
        rounded = (x_ref[:, cols].astype(f32) + acc).astype(bf16)
        res_ref[:, cols] = rounded
        wide = rounded.astype(f32)
        total = total + jnp.sum(wide * wide, axis=-1, keepdims=True)
    factor = lax.rsqrt(total / D + norm_eps)
    for cols in columns():
        wide = res_ref[:, cols].astype(f32)
        rows = (wide * factor * gain_ref[:, cols].astype(f32)).astype(bf16)
        ffn_ref[:, cols] = rows
        slots = jnp.dot(sel.astype(bf16), rows, preferred_element_type=f32).astype(bf16)
        for dest in range(EP):
            copies_ref[dest, :, cols] = slots
    logits = dot_last(router_ref[...], ffn_ref[...])
    expert = lax.broadcasted_iota(jnp.int32, (EXPERTS, TOK), 0)
    pick_one = jnp.sum(jnp.where(expert == one, logits, 0.0), axis=0, keepdims=True)
    pick_two = jnp.sum(jnp.where(expert == two, logits, 0.0), axis=0, keepdims=True)
    top = jnp.maximum(pick_one, pick_two)
    e_one = jnp.exp(pick_one - top)
    e_two = jnp.exp(pick_two - top)
    both = e_one + e_two
    share = jnp.where(one == 0, e_one / both, 0.0) + jnp.where(two == 0, e_two / both, 0.0)
    coef_ref[...] = share * sel


def expert_body(x_ref, gate_ref, up_ref, down_ref, part_ref):
    x = x_ref[...]
    gate = dot_last(x, gate_ref[...])
    up = dot_last(x, up_ref[...])
    hidden = (gate * jax.nn.sigmoid(gate) * up).astype(bf16)
    part_ref[...] = jnp.dot(hidden, down_ref[0], preferred_element_type=f32).astype(bf16)


def combine_body(res_ref, coef_ref, got_ref, out_ref):
    coef = coef_ref[...]
    for cols in columns():
        acc = got_ref[0, :, cols].astype(f32)
        for src in range(1, EP):
            acc = acc + got_ref[src, :, cols].astype(f32)
        out_ref[:, cols] = (res_ref[:, cols].astype(f32) + dot_first(coef, acc)).astype(bf16)


def sds(shape, dtype):
    return jax.ShapeDtypeStruct(shape, dtype)


def trade(pieces):
    return lax.all_to_all(pieces, "ep", split_axis=0, concat_axis=0, tiled=True)


def local(
    states,
    entering,
    seq_lens,
    routes,
    attn_norm,
    ffn_norm,
    wq,
    wk,
    wv,
    wo,
    router,
    w_gate,
    w_up,
    w_down,
    cache_k,
    cache_v,
    k_scale,
    v_scale,
):
    rotary = rotary_table()
    ks = jnp.transpose(k_scale[0], (0, 2, 3, 1))
    vs = jnp.transpose(v_scale[0], (0, 2, 3, 1))
    chosen = jnp.transpose(routes[0], (0, 2, 1))
    wk_t, wv_t, router_t, gate_t, up_t = (
        jnp.transpose(w[0], (1, 0)) for w in (wk, wv, router, w_gate, w_up)
    )

    turn = turn_of()
    ep_index = lax.axis_index("ep")
    sections = lax.axis_size("section")
    sent_depth = ((ep_index >> 2) + turn + 1) % 2 * HALF
    sent_cols = (ep_index + turn + 1) % 2 * HALF
    both = ("section", "ep")
    sent_wo = lax.dynamic_slice(wo[0], (0, sent_cols), (256, HALF))
    sent_q = lax.dynamic_slice(wq[0], (sent_depth, 0), (HALF, 256))
    sent_kv = jnp.concatenate(
        [lax.dynamic_slice(w, (0, sent_depth), (64, HALF)) for w in (wk_t, wv_t)], axis=0
    )
    others = (
        lax.ppermute(sent_wo, both, partner_list("x", sections)),
        lax.ppermute(sent_q, both, partner_list("y", sections)),
        lax.ppermute(sent_kv, both, partner_list("y", sections)),
    )

    copies = call(
        norm_body,
        sds((EP, TOK, D), bf16),
        2,
        name="norm",
        scratch=[
            pltpu.VMEM((TOK, D), bf16),
            pltpu.VMEM((1, D), bf16),
            pltpu.SemaphoreType.DMA((2,)),
        ],
        space=pltpu.HBM,
    )(states, attn_norm)
    everyone = trade(copies)
    projected = call(project_body, sds((EP * TOK, QKV), bf16), 4, name="project")(
        everyone.reshape(EP * TOK, D), wq[0], wk_t, wv_t
    )

    def run_layer(x, projected, tick, others):
        got = trade(projected.reshape(EP, TOK, projected.shape[1]))
        attended = call(
            functools.partial(attention_body, tick),
            sds((EP, TOK, 512), bf16),
            7,
            name="attend",
        )(got, seq_lens, rotary, ks, vs, cache_k, cache_v)
        if tick == 0:
            attended, *others = lax.optimization_barrier((attended, *others))
        heads = trade(attended)
        part = call(out_body, sds((EP * TOK, HALF), bf16), 3, name="outproj")(
            heads.reshape(EP * TOK, 512), wo, others[0]
        )
        sums = trade(part.reshape(EP, TOK, HALF))
        residual, slots, coef = call(
            functools.partial(residual_body, tick),
            (sds((TOK, D), bf16), sds((EP, CAP, D), bf16), sds((CAP, TOK), f32)),
            5,
            name="residual",
            scratch=[pltpu.VMEM((TOK, D), bf16)],
        )(x, sums, ffn_norm, router_t, chosen)
        landed = trade(slots).reshape(EP * CAP, D)
        pieces = call(expert_body, sds((EP * CAP, D), bf16), 4, name="expert", limit=16)(
            landed, gate_t, up_t, w_down
        )
        returned = trade(pieces.reshape(EP, CAP, D))
        out = call(combine_body, sds((TOK, D), bf16), 3, name="combine")(residual, coef, returned)
        return out, others

    first_out, others = run_layer(states, projected, 0, others)
    shifted = lax.ppermute(first_out, "section", [(i, i + 1) for i in range(sections - 1)])
    second_in, copies = call(
        norm_select_body,
        (sds((TOK, D), bf16), sds((EP, TOK, HALF), bf16)),
        3,
        name="select_norm",
    )(entering, shifted, attn_norm)
    everyone = trade(copies).reshape(EP * TOK, HALF)
    projected = call(project_halves_body, sds((EP * TOK, 2 * QKV), bf16), 6, name="project2")(
        everyone, wq[0], wk_t, wv_t, others[1], others[2]
    )
    return run_layer(second_in, projected, 1, others)[0]


def solution(mesh):
    return jax.shard_map(
        local,
        mesh=mesh,
        in_specs=(
            P(("section", "ep"), None),
            P("ep", None),
            P(),
            P("section", None, "ep", None),
            P("section", None),
            P("section", None),
            P("section", None, "ep"),
            P("section", None, "ep"),
            P("section", None, "ep"),
            P("section", "ep", None),
            P("section", None, None),
            P("section", None, "ep"),
            P("section", None, "ep"),
            P("section", "ep", None),
            P("section", None, "ep", None, None, None),
            P("section", None, "ep", None, None, None),
            P("section", None, "ep", None, None),
            P("section", None, "ep", None, None),
        ),
        out_specs=P(("section", "ep"), None),
        check_vma=False,
    )
```

```python
import functools

import jax
import jax.numpy as jnp
import numpy as np
from jax import lax
from jax.experimental import pallas as pl
from jax.experimental.pallas import tpu as pltpu
from jax.sharding import PartitionSpec as P

D = 3072
QH = 32
KVH = 8
HD = 128
EXPERTS = 8
EXP_WIN = 1
LEN = 16
BLK = 4
CAP = 8
EP = 16
TOK = 16
CHUNK = 512
HALF = D // 2
QKV = 384

rope_base = 1000000.0
norm_eps = 1e-05
f32 = jnp.float32
bf16 = jnp.bfloat16


def call(body, out_shape, n_in, far=(), far_out=False, name=None, scratch=(), limit=4):
    specs = [
        pl.BlockSpec(memory_space=pl.ANY if i in far else pltpu.VMEM) for i in range(n_in)
    ]
    space = pl.ANY if far_out else pltpu.VMEM
    outs = jax.tree.map(lambda _: pl.BlockSpec(memory_space=space), out_shape)
    return pl.pallas_call(
        body,
        out_shape=out_shape,
        in_specs=specs,
        out_specs=outs,
        scratch_shapes=list(scratch),
        compiler_params=pltpu.CompilerParams(vmem_limit_bytes=limit << 20),
        name=name,
    )


def dot_last(left, right):
    return lax.dot_general(left, right, (((1,), (1,)), ((), ())), preferred_element_type=f32)


def dot_first(left, right):
    return lax.dot_general(
        left,
        right,
        (((0,), (0,)), ((), ())),
        preferred_element_type=f32,
        precision=lax.Precision.HIGHEST,
    )


def columns():
    return [slice(c, c + CHUNK) for c in range(0, D, CHUNK)]


def turn_of():
    return lax.axis_index("section") & 1


def x_partner(device, turn):
    x = device & 3
    odd = ((((x + 1) & 3) ^ 1) + 3) & 3
    return (device - x) + jnp.where(turn == 0, x ^ 1, odd)


def y_partner(device, turn):
    y = device >> 2
    odd = ((((y + 1) & 3) ^ 1) + 3) & 3
    return (device & 3) + 4 * jnp.where(turn == 0, y ^ 1, odd)


def partner_list(partner, sections):
    def odd_pair(v):
        return ((((v + 1) & 3) ^ 1) + 3) & 3

    pairs = []
    for section in range(sections):
        for device in range(EP):
            y, x = divmod(device, 4)
            if partner == "x":
                x = x ^ 1 if section % 2 == 0 else odd_pair(x)
            else:
                y = y ^ 1 if section % 2 == 0 else odd_pair(y)
            pairs.append((section * EP + device, section * EP + 4 * y + x))
    return pairs


def spread_halves(x_ref, gain_ref, copies_ref):
    total = jnp.zeros((TOK, 1), f32)
    for cols in columns():
        wide = x_ref[:, cols].astype(f32)
        total = total + jnp.sum(wide * wide, axis=-1, keepdims=True)
    factor = lax.rsqrt(total / D + norm_eps)
    turn = turn_of()
    for cols in columns():
        wide = x_ref[:, cols].astype(f32)
        rows = (wide * factor * gain_ref[:, cols].astype(f32)).astype(bf16)
        part = cols.start // HALF
        kept = slice(cols.start - part * HALF, cols.stop - part * HALF)
        for k in range(2):
            for x in range(4):
                copies_ref[(2 * k + (turn ^ part)) * 4 + x, :, kept] = rows


def norm_body(x_ref, gain_ref, copies_hbm, rows_ref, sems):
    total = jnp.zeros((TOK, 1), f32)
    for cols in columns():
        wide = x_ref[:, cols].astype(f32)
        total = total + jnp.sum(wide * wide, axis=-1, keepdims=True)
    factor = lax.rsqrt(total / D + norm_eps)
    for cols in columns():
        wide = x_ref[:, cols].astype(f32)
        rows_ref[:, cols] = (wide * factor * gain_ref[:, cols].astype(f32)).astype(bf16)
    sends = [
        pltpu.make_async_copy(rows_ref, copies_hbm.at[dest], sems.at[dest]) for dest in range(EP)
    ]
    for send in sends:
        send.start()
    for send in sends:
        send.wait()


def norm_select_body(entering_ref, shifted_ref, gain_ref, x_ref, copies_ref):
    is_first = lax.axis_index("section") == 0

    @pl.when(is_first)
    def _():
        x_ref[...] = entering_ref[...]

    @pl.when(jnp.logical_not(is_first))
    def _():
        x_ref[...] = shifted_ref[...]

    spread_halves(x_ref, gain_ref, copies_ref)


def project_body(x_ref, wq_ref, kv_ref, out_ref):
    x = x_ref[...]
    out_ref[:, 0:256] = jnp.dot(x, wq_ref[...], preferred_element_type=f32).astype(bf16)
    out_ref[:, 256:QKV] = dot_last(x, kv_ref[...]).astype(bf16)


def project_halves_body(x_ref, own_q_ref, own_kv_ref, q_ref, kv_ref, out_ref):
    x = x_ref[...]
    out_ref[:, 0:256] = jnp.dot(x, own_q_ref[...], preferred_element_type=f32).astype(bf16)
    out_ref[:, 256:QKV] = dot_last(x, own_kv_ref[...]).astype(bf16)
    out_ref[:, QKV : QKV + 256] = jnp.dot(x, q_ref[...], preferred_element_type=f32).astype(bf16)
    out_ref[:, QKV + 256 : 2 * QKV] = dot_last(x, kv_ref[...]).astype(bf16)


def rotary_table():
    half = HD // 2
    inv_freq = rope_base ** (-np.arange(half, dtype=np.float64) * 2.0 / HD)
    angles = np.arange(2 * LEN, dtype=np.float64)[:, None] * inv_freq
    cos_vals, sin_vals = np.cos(angles), np.sin(angles)
    return np.concatenate([cos_vals, cos_vals, -sin_vals, sin_vals], axis=1).astype(np.float32)


def attention_body(
    tick, got_ref, lens_ref, rotary_ref, ks_ref, vs_ref, key_ref, value_ref, out_ref
):
    scale = HD ** (-0.5)
    group = QH // KVH
    pos = TOK * LEN
    lane = lax.broadcasted_iota(jnp.int32, (TOK, HD), 1)
    low = lane < HD // 2
    turn = turn_of()

    def rows_of(src, start, stop):
        rows = got_ref[src, :, start:stop].astype(f32)
        if tick == 1:
            other = got_ref[y_partner(src, turn), :, QKV + start : QKV + stop].astype(f32)
            rows = (rows + other).astype(bf16).astype(f32)
        return rows

    row_lens = lens_ref[pl.ds(lax.axis_index("section") + 1 - tick, 1), :].astype(f32)
    mine = lax.broadcasted_iota(jnp.int32, (TOK, row_lens.shape[1]), 0) + lax.axis_index("ep") * TOK
    there = lax.broadcasted_iota(jnp.int32, (TOK, row_lens.shape[1]), 1)
    lens = jnp.sum(jnp.where(mine == there, row_lens, 0.0), axis=-1, keepdims=True)
    lens = lens.astype(jnp.int32)
    length = lax.broadcasted_iota(jnp.int32, (TOK, 2 * LEN), 1)
    rotary = jnp.dot(
        jnp.where(length == lens, 1.0, 0.0).astype(f32),
        rotary_ref[...],
        preferred_element_type=f32,
        precision=lax.Precision.HIGHEST,
    )
    cos_vals = rotary[:, 0:HD]
    sin_vals = rotary[:, HD : 2 * HD]

    def turned(rows):
        return (rows * cos_vals + pltpu.roll(rows, HD // 2, 1) * sin_vals).astype(bf16)

    blocks = LEN // BLK
    which = lax.broadcasted_iota(jnp.int32, (KVH * blocks, KVH * pos), 0)
    at = lax.broadcasted_iota(jnp.int32, (KVH * blocks, KVH * pos), 1)
    spread = jnp.where(
        (which // blocks == at // pos) & (which % blocks == (at % LEN) // BLK), 1.0, 0.0
    ).astype(f32)
    k_all = dot_first(jnp.concatenate([ks_ref[tick, g] for g in range(KVH)], axis=0), spread)
    v_all = dot_first(jnp.concatenate([vs_ref[tick, g] for g in range(KVH)], axis=0), spread)
    row = lax.broadcasted_iota(jnp.int32, (TOK, pos), 0)
    col = lax.broadcasted_iota(jnp.int32, (TOK, pos), 1)
    live_one = (col // LEN == row) & (col % LEN < lens)
    live = jnp.concatenate([live_one.astype(f32)] * group, axis=0) > 0.5
    for g in range(KVH):
        first = rows_of(2 * g, 256, QKV)
        second = rows_of(2 * g + 1, 256, QKV)
        key_new = turned(jnp.where(low, first, pltpu.roll(second, HD // 2, 1))).astype(f32)
        value_new = jnp.where(low, pltpu.roll(first, HD // 2, 1), second)
        q = jnp.concatenate(
            [
                turned(rows_of(2 * g + r // 2, (r % 2) * HD, (r % 2 + 1) * HD))
                for r in range(group)
            ],
            axis=0,
        )
        keys = key_ref[0, tick, :, g].reshape(pos, HD)
        values = value_ref[0, tick, :, g].reshape(pos, HD)
        k_scale = jnp.concatenate([k_all[:, g * pos : (g + 1) * pos]] * group, axis=0)
        v_scale = jnp.concatenate([v_all[:, g * pos : (g + 1) * pos]] * group, axis=0)
        scores = dot_last(q, keys) * k_scale * scale
        own = (
            jnp.sum(
                q.astype(f32) * jnp.concatenate([key_new] * group, axis=0), axis=-1, keepdims=True
            )
            * scale
        )
        top = jnp.maximum(jnp.max(jnp.where(live, scores, -1e30), axis=-1, keepdims=True), own)
        e = jnp.where(live, jnp.exp(jnp.where(live, scores, -1e30) - top), 0.0)
        e_own = jnp.exp(own - top)
        denom = jnp.sum(e, axis=-1, keepdims=True) + e_own
        weight = jnp.where(live, e * v_scale, 0.0).astype(bf16)
        mixed = jnp.dot(weight, values, preferred_element_type=f32)
        mixed = mixed + e_own * jnp.concatenate([value_new] * group, axis=0)
        done = (mixed / denom).astype(bf16)
        for r in range(group):
            rows = done[r * TOK : (r + 1) * TOK]
            at = (r % 2) * HD
            owner = 2 * g + r // 2
            out_ref[owner, :, at : at + HD] = rows
            out_ref[x_partner(owner, turn), :, 256 + at : 256 + at + HD] = rows


def out_body(att_ref, wo_ref, other_ref, part_ref):
    total = jnp.dot(att_ref[:, 0:256], wo_ref[...], preferred_element_type=f32)
    total = total + jnp.dot(att_ref[:, 256:512], other_ref[...], preferred_element_type=f32)
    part_ref[...] = total.astype(bf16)


def out_fetch_body(att_ref, wo_ref, *refs):
    swapped, part_ref, fetched, sems = refs[:3], refs[3], refs[4:7], refs[7]
    fetches = [
        pltpu.make_async_copy(there, here, sems.at[i])
        for i, (there, here) in enumerate(zip(swapped, fetched))
    ]
    for fetch in fetches:
        fetch.start()
    fetches[0].wait()
    out_body(att_ref, wo_ref, fetched[0], part_ref)
    for fetch in fetches[1:]:
        fetch.wait()


def residual_body(
    tick, x_ref, got_ref, gain_ref, router_ref, chosen_ref, res_ref, copies_ref, coef_ref, ffn_ref
):
    one = chosen_ref[tick, 0:1, :]
    two = chosen_ref[tick, 1:2, :]
    held = jnp.where((one == 0) | (two == 0), 1.0, 0.0).astype(f32)
    held = jnp.broadcast_to(held, (CAP, TOK))
    before = lax.broadcasted_iota(jnp.int32, (TOK, TOK), 0) < lax.broadcasted_iota(
        jnp.int32, (TOK, TOK), 1
    )
    rank = jnp.dot(
        held.astype(bf16), before.astype(f32).astype(bf16), preferred_element_type=f32
    )
    slot = lax.broadcasted_iota(jnp.int32, (CAP, TOK), 0).astype(f32)
    sel = jnp.where((held > 0.5) & (rank == slot), 1.0, 0.0).astype(f32)
    total = jnp.zeros((TOK, 1), f32)
    for cols in columns():
        part = cols.start // HALF
        held_cols = slice(cols.start - part * HALF, cols.stop - part * HALF)
        first = turn_of() ^ part
        acc = got_ref[first, :, held_cols].astype(f32)
        for pair in range(1, EP // 2):
            acc = acc + got_ref[2 * pair + first, :, held_cols].astype(f32)
        rounded = (x_ref[:, cols].astype(f32) + acc).astype(bf16)
        res_ref[:, cols] = rounded
        wide = rounded.astype(f32)
        total = total + jnp.sum(wide * wide, axis=-1, keepdims=True)
    factor = lax.rsqrt(total / D + norm_eps)
    for cols in columns():
        wide = res_ref[:, cols].astype(f32)
        rows = (wide * factor * gain_ref[:, cols].astype(f32)).astype(bf16)
        ffn_ref[:, cols] = rows
        slots = jnp.dot(sel.astype(bf16), rows, preferred_element_type=f32).astype(bf16)
        for dest in range(EP):
            copies_ref[dest, :, cols] = slots
    logits = dot_last(router_ref[...], ffn_ref[...])
    expert = lax.broadcasted_iota(jnp.int32, (EXPERTS, TOK), 0)
    pick_one = jnp.sum(jnp.where(expert == one, logits, 0.0), axis=0, keepdims=True)
    pick_two = jnp.sum(jnp.where(expert == two, logits, 0.0), axis=0, keepdims=True)
    top = jnp.maximum(pick_one, pick_two)
    e_one = jnp.exp(pick_one - top)
    e_two = jnp.exp(pick_two - top)
    both = e_one + e_two
    share = jnp.where(one == 0, e_one / both, 0.0) + jnp.where(two == 0, e_two / both, 0.0)
    coef_ref[...] = share * sel


def expert_body(x_ref, gate_ref, up_ref, down_ref, part_ref):
    x = x_ref[...]
    gate = dot_last(x, gate_ref[...])
    up = dot_last(x, up_ref[...])
    hidden = (gate * jax.nn.sigmoid(gate) * up).astype(bf16)
    part_ref[...] = jnp.dot(hidden, down_ref[0], preferred_element_type=f32).astype(bf16)


def combine_body(res_ref, coef_ref, got_ref, out_ref):
    coef = coef_ref[...]
    for cols in columns():
        acc = got_ref[0, :, cols].astype(f32)
        for src in range(1, EP):
            acc = acc + got_ref[src, :, cols].astype(f32)
        out_ref[:, cols] = (res_ref[:, cols].astype(f32) + dot_first(coef, acc)).astype(bf16)


def sds(shape, dtype):
    return jax.ShapeDtypeStruct(shape, dtype)


def trade(pieces):
    return lax.all_to_all(pieces, "ep", split_axis=0, concat_axis=0, tiled=True)


def local(
    states,
    entering,
    seq_lens,
    routes,
    attn_norm,
    ffn_norm,
    wq,
    wk,
    wv,
    wo,
    router,
    w_gate,
    w_up,
    w_down,
    cache_k,
    cache_v,
    k_scale,
    v_scale,
):
    rotary = rotary_table()
    ks = jnp.transpose(k_scale[0], (0, 2, 3, 1))
    vs = jnp.transpose(v_scale[0], (0, 2, 3, 1))
    chosen = jnp.transpose(routes[0], (0, 2, 1))
    wk_t, wv_t, router_t, gate_t, up_t = (
        jnp.transpose(w[0], (1, 0)) for w in (wk, wv, router, w_gate, w_up)
    )

    turn = turn_of()
    ep_index = lax.axis_index("ep")
    sections = lax.axis_size("section")
    sent_depth = ((ep_index >> 2) + turn + 1) % 2 * HALF
    sent_cols = (ep_index + turn + 1) % 2 * HALF
    both = ("section", "ep")
    kv = jnp.concatenate([wk_t, wv_t], axis=0)
    sent_wo = lax.dynamic_slice(wo[0], (0, sent_cols), (256, HALF))
    sent_q = lax.dynamic_slice(wq[0], (sent_depth, 0), (HALF, 256))
    sent_kv = lax.dynamic_slice(kv, (0, sent_depth), (128, HALF))
    own_wo = lax.dynamic_slice(wo[0], (0, HALF - sent_cols), (256, HALF))
    own_q = lax.dynamic_slice(wq[0], (HALF - sent_depth, 0), (HALF, 256))
    own_kv = lax.dynamic_slice(kv, (0, HALF - sent_depth), (128, HALF))
    others = (
        lax.ppermute(sent_wo, both, partner_list("x", sections)),
        lax.ppermute(sent_q, both, partner_list("y", sections)),
        lax.ppermute(sent_kv, both, partner_list("y", sections)),
    )

    copies = call(
        norm_body,
        sds((EP, TOK, D), bf16),
        2,
        far_out=True,
        name="norm",
        scratch=[pltpu.VMEM((TOK, D), bf16), pltpu.SemaphoreType.DMA((EP,))],
    )(states, attn_norm)
    everyone, kv, own_wo, own_q, own_kv = lax.optimization_barrier(
        (trade(copies).reshape(EP * TOK, D), kv, own_wo, own_q, own_kv)
    )
    projected = call(project_body, sds((EP * TOK, QKV), bf16), 3, name="project", limit=6)(
        everyone, wq[0], kv
    )

    def run_layer(x, projected, tick, others):
        got = trade(projected.reshape(EP, TOK, projected.shape[1]))
        attended = call(
            functools.partial(attention_body, tick), sds((EP, TOK, 512), bf16), 7, name="attend"
        )(got, seq_lens, rotary, ks, vs, cache_k, cache_v)
        part = sds((EP * TOK, HALF), bf16)
        if tick == 0:
            attended, *others = lax.optimization_barrier((attended, *others))
            heads = trade(attended).reshape(EP * TOK, 512)
            part, *others = call(
                out_fetch_body,
                (part, *(sds(o.shape, bf16) for o in others)),
                5,
                far=(2, 3, 4),
                name="outproj",
                scratch=[pltpu.SemaphoreType.DMA((3,))],
            )(heads, own_wo, *others)
        else:
            heads = trade(attended).reshape(EP * TOK, 512)
            part = call(out_body, part, 3, name="outproj")(heads, own_wo, others[0])
        sums = trade(part.reshape(EP, TOK, HALF))
        residual, slots, coef = call(
            functools.partial(residual_body, tick),
            (sds((TOK, D), bf16), sds((EP, CAP, D), bf16), sds((CAP, TOK), f32)),
            5,
            name="residual",
            scratch=[pltpu.VMEM((TOK, D), bf16)],
        )(x, sums, ffn_norm, router_t, chosen)
        landed = trade(slots).reshape(EP * CAP, D)
        pieces = call(expert_body, sds((EP * CAP, D), bf16), 4, name="expert", limit=8)(
            landed, gate_t, up_t, w_down
        )
        returned = trade(pieces.reshape(EP, CAP, D))
        out = call(combine_body, sds((TOK, D), bf16), 3, name="combine")(residual, coef, returned)
        return out, others

    first_out, others = run_layer(states, projected, 0, others)
    shifted = lax.ppermute(first_out, "section", [(i, i + 1) for i in range(sections - 1)])
    second_in, copies = call(
        norm_select_body,
        (sds((TOK, D), bf16), sds((EP, TOK, HALF), bf16)),
        3,
        name="select_norm",
    )(entering, shifted, attn_norm)
    everyone = trade(copies).reshape(EP * TOK, HALF)
    projected = call(project_halves_body, sds((EP * TOK, 2 * QKV), bf16), 5, name="project2")(
        everyone, own_q, own_kv, others[1], others[2]
    )
    return run_layer(second_in, projected, 1, others)[0]


def solution(mesh):
    return jax.shard_map(
        local,
        mesh=mesh,
        in_specs=(
            P(("section", "ep"), None),
            P("ep", None),
            P(),
            P("section", None, "ep", None),
            P("section", None),
            P("section", None),
            P("section", None, "ep"),
            P("section", None, "ep"),
            P("section", None, "ep"),
            P("section", "ep", None),
            P("section", None, None),
            P("section", None, "ep"),
            P("section", None, "ep"),
            P("section", "ep", None),
            P("section", None, "ep", None, None, None),
            P("section", None, "ep", None, None, None),
            P("section", None, "ep", None, None),
            P("section", None, "ep", None, None),
        ),
        out_specs=P(("section", "ep"), None),
        check_vma=False,
    )
```

```python
import functools

import jax
import jax.numpy as jnp
import numpy as np
from jax import lax
from jax.experimental import pallas as pl
from jax.experimental.pallas import tpu as pltpu
from jax.sharding import PartitionSpec as P

D = 3072
QH = 32
KVH = 8
HD = 128
EXPERTS = 8
EXP_WIN = 1
LEN = 16
BLK = 4
CAP = 8
EP = 16
TOK = 16
CHUNK = 512
HALF = D // 2
QKV = 384

rope_base = 1000000.0
norm_eps = 1e-05
f32 = jnp.float32
bf16 = jnp.bfloat16


def call(body, out_shape, n_in, far=(), far_out=False, name=None, scratch=(), limit=4):
    specs = [
        pl.BlockSpec(memory_space=pl.ANY if i in far else pltpu.VMEM) for i in range(n_in)
    ]
    space = pl.ANY if far_out else pltpu.VMEM
    outs = jax.tree.map(lambda _: pl.BlockSpec(memory_space=space), out_shape)
    return pl.pallas_call(
        body,
        out_shape=out_shape,
        in_specs=specs,
        out_specs=outs,
        scratch_shapes=list(scratch),
        compiler_params=pltpu.CompilerParams(vmem_limit_bytes=limit << 20),
        name=name,
    )


def dot_last(left, right):
    return lax.dot_general(left, right, (((1,), (1,)), ((), ())), preferred_element_type=f32)


def dot_first(left, right):
    return lax.dot_general(
        left,
        right,
        (((0,), (0,)), ((), ())),
        preferred_element_type=f32,
        precision=lax.Precision.HIGHEST,
    )


def columns():
    return [slice(c, c + CHUNK) for c in range(0, D, CHUNK)]


def turn_of():
    return lax.axis_index("section") & 1


def x_partner(device, turn):
    x = device & 3
    odd = ((((x + 1) & 3) ^ 1) + 3) & 3
    return (device - x) + jnp.where(turn == 0, x ^ 1, odd)


def y_partner(device, turn):
    y = device >> 2
    odd = ((((y + 1) & 3) ^ 1) + 3) & 3
    return (device & 3) + 4 * jnp.where(turn == 0, y ^ 1, odd)


def partner_list(partner, sections):
    def odd_pair(v):
        return ((((v + 1) & 3) ^ 1) + 3) & 3

    pairs = []
    for section in range(sections):
        for device in range(EP):
            y, x = divmod(device, 4)
            if partner == "x":
                x = x ^ 1 if section % 2 == 0 else odd_pair(x)
            else:
                y = y ^ 1 if section % 2 == 0 else odd_pair(y)
            pairs.append((section * EP + device, section * EP + 4 * y + x))
    return pairs


def spread_halves(x_ref, gain_ref, copies_ref):
    total = jnp.zeros((TOK, 1), f32)
    for cols in columns():
        wide = x_ref[:, cols].astype(f32)
        total = total + jnp.sum(wide * wide, axis=-1, keepdims=True)
    factor = lax.rsqrt(total / D + norm_eps)
    turn = turn_of()
    for cols in columns():
        wide = x_ref[:, cols].astype(f32)
        rows = (wide * factor * gain_ref[:, cols].astype(f32)).astype(bf16)
        part = cols.start // HALF
        kept = slice(cols.start - part * HALF, cols.stop - part * HALF)
        for k in range(2):
            for x in range(4):
                copies_ref[(2 * k + (turn ^ part)) * 4 + x, :, kept] = rows


def norm_body(x_ref, gain_ref, copies_hbm, rows_ref, sems):
    total = jnp.zeros((TOK, 1), f32)
    for cols in columns():
        wide = x_ref[:, cols].astype(f32)
        total = total + jnp.sum(wide * wide, axis=-1, keepdims=True)
    factor = lax.rsqrt(total / D + norm_eps)
    for cols in columns():
        wide = x_ref[:, cols].astype(f32)
        rows_ref[:, cols] = (wide * factor * gain_ref[:, cols].astype(f32)).astype(bf16)
    sends = [
        pltpu.make_async_copy(rows_ref, copies_hbm.at[dest], sems.at[dest]) for dest in range(EP)
    ]
    for send in sends:
        send.start()
    for send in sends:
        send.wait()


def norm_select_body(entering_ref, shifted_ref, gain_ref, x_ref, copies_ref):
    is_first = lax.axis_index("section") == 0

    @pl.when(is_first)
    def _():
        x_ref[...] = entering_ref[...]

    @pl.when(jnp.logical_not(is_first))
    def _():
        x_ref[...] = shifted_ref[...]

    spread_halves(x_ref, gain_ref, copies_ref)


def project_body(x_ref, joined_ref, out_ref):
    out_ref[...] = jnp.dot(x_ref[...], joined_ref[...], preferred_element_type=f32).astype(bf16)


def project_halves_body(x_ref, own_ref, other_ref, out_ref):
    x = x_ref[...]
    out_ref[:, 0:QKV] = jnp.dot(x, own_ref[...], preferred_element_type=f32).astype(bf16)
    out_ref[:, QKV : 2 * QKV] = jnp.dot(x, other_ref[...], preferred_element_type=f32).astype(bf16)


def rotary_table():
    half = HD // 2
    inv_freq = rope_base ** (-np.arange(half, dtype=np.float64) * 2.0 / HD)
    angles = np.arange(2 * LEN, dtype=np.float64)[:, None] * inv_freq
    cos_vals, sin_vals = np.cos(angles), np.sin(angles)
    return np.concatenate([cos_vals, cos_vals, -sin_vals, sin_vals], axis=1).astype(np.float32)


def attention_body(
    tick, got_ref, lens_ref, rotary_ref, ks_ref, vs_ref, key_ref, value_ref, out_ref
):
    scale = HD ** (-0.5)
    group = QH // KVH
    pos = TOK * LEN
    lane = lax.broadcasted_iota(jnp.int32, (TOK, HD), 1)
    low = lane < HD // 2
    turn = turn_of()

    def rows_of(src, start, stop):
        rows = got_ref[src, :, start:stop].astype(f32)
        if tick == 1:
            other = got_ref[y_partner(src, turn), :, QKV + start : QKV + stop].astype(f32)
            rows = (rows + other).astype(bf16).astype(f32)
        return rows

    row_lens = lens_ref[pl.ds(lax.axis_index("section") + 1 - tick, 1), :].astype(f32)
    mine = lax.broadcasted_iota(jnp.int32, (TOK, row_lens.shape[1]), 0) + lax.axis_index("ep") * TOK
    there = lax.broadcasted_iota(jnp.int32, (TOK, row_lens.shape[1]), 1)
    lens = jnp.sum(jnp.where(mine == there, row_lens, 0.0), axis=-1, keepdims=True)
    lens = lens.astype(jnp.int32)
    length = lax.broadcasted_iota(jnp.int32, (TOK, 2 * LEN), 1)
    rotary = jnp.dot(
        jnp.where(length == lens, 1.0, 0.0).astype(f32),
        rotary_ref[...],
        preferred_element_type=f32,
        precision=lax.Precision.HIGHEST,
    )
    cos_vals = rotary[:, 0:HD]
    sin_vals = rotary[:, HD : 2 * HD]

    def turned(rows):
        return (rows * cos_vals + pltpu.roll(rows, HD // 2, 1) * sin_vals).astype(bf16)

    blocks = LEN // BLK
    eye = lax.broadcasted_iota(jnp.int32, (KVH * blocks, KVH * blocks), 0)
    eye = (eye == lax.broadcasted_iota(jnp.int32, (KVH * blocks, KVH * blocks), 1)).astype(f32)
    k_rows = dot_first(jnp.concatenate([ks_ref[tick, g] for g in range(KVH)], axis=0), eye)
    v_rows = dot_first(jnp.concatenate([vs_ref[tick, g] for g in range(KVH)], axis=0), eye)
    block_at = lane % LEN // BLK

    def spread(rows, g):
        wide = jnp.broadcast_to(rows[:, g * blocks : g * blocks + 1], (TOK, HD))
        for k in range(1, blocks):
            at = g * blocks + k
            wide = jnp.where(block_at == k, rows[:, at : at + 1], wide)
        one = jnp.concatenate([wide] * (pos // HD), axis=1)
        return jnp.concatenate([one] * group, axis=0)

    row = lax.broadcasted_iota(jnp.int32, (TOK, pos), 0)
    col = lax.broadcasted_iota(jnp.int32, (TOK, pos), 1)
    live_one = (col // LEN == row) & (col % LEN < lens)
    live = jnp.concatenate([live_one.astype(f32)] * group, axis=0) > 0.5
    heads = range(KVH)
    queries, fresh_keys, fresh_values, scores = [], [], [], []
    for g in heads:
        first = rows_of(2 * g, 256, QKV)
        second = rows_of(2 * g + 1, 256, QKV)
        key_new = turned(jnp.where(low, first, pltpu.roll(second, HD // 2, 1))).astype(f32)
        fresh_keys.append(key_new)
        fresh_values.append(jnp.where(low, pltpu.roll(first, HD // 2, 1), second))
        q = jnp.concatenate(
            [
                turned(rows_of(2 * g + r // 2, (r % 2) * HD, (r % 2 + 1) * HD))
                for r in range(group)
            ],
            axis=0,
        )
        queries.append(q)
        scores.append(dot_last(q, key_ref[0, tick, :, g].reshape(pos, HD)))
    weights, owns, denoms = [], [], []
    for g in heads:
        score = jnp.where(live, scores[g] * spread(k_rows, g) * scale, -1e30)
        own = (
            jnp.sum(
                queries[g].astype(f32) * jnp.concatenate([fresh_keys[g]] * group, axis=0),
                axis=-1,
                keepdims=True,
            )
            * scale
        )
        top = jnp.maximum(jnp.max(score, axis=-1, keepdims=True), own)
        e = jnp.where(live, jnp.exp(score - top), 0.0)
        e_own = jnp.exp(own - top)
        owns.append(e_own)
        denoms.append(jnp.sum(e, axis=-1, keepdims=True) + e_own)
        weights.append((e * spread(v_rows, g)).astype(bf16))
    mixes = [
        jnp.dot(
            weights[g], value_ref[0, tick, :, g].reshape(pos, HD), preferred_element_type=f32
        )
        for g in heads
    ]
    for g in heads:
        mixed = mixes[g] + owns[g] * jnp.concatenate([fresh_values[g]] * group, axis=0)
        done = (mixed / denoms[g]).astype(bf16)
        for r in range(group):
            rows = done[r * TOK : (r + 1) * TOK]
            at = (r % 2) * HD
            owner = 2 * g + r // 2
            out_ref[owner, :, at : at + HD] = rows
            out_ref[x_partner(owner, turn), :, 256 + at : 256 + at + HD] = rows


def out_body(att_ref, wo_ref, other_ref, part_ref):
    total = jnp.dot(att_ref[:, 0:256], wo_ref[...], preferred_element_type=f32)
    total = total + jnp.dot(att_ref[:, 256:512], other_ref[...], preferred_element_type=f32)
    part_ref[...] = total.astype(bf16)


def out_fetch_body(att_ref, wo_ref, *refs):
    swapped, part_ref, fetched, sems = refs[:2], refs[2], refs[3:5], refs[5]
    fetches = [
        pltpu.make_async_copy(there, here, sems.at[i])
        for i, (there, here) in enumerate(zip(swapped, fetched))
    ]
    for fetch in fetches:
        fetch.start()
    fetches[0].wait()
    out_body(att_ref, wo_ref, fetched[0], part_ref)
    for fetch in fetches[1:]:
        fetch.wait()


def residual_body(
    tick, x_ref, got_ref, gain_ref, router_ref, chosen_ref, res_ref, copies_ref, coef_ref, ffn_ref
):
    one = chosen_ref[tick, 0:1, :]
    two = chosen_ref[tick, 1:2, :]
    held = jnp.where((one == 0) | (two == 0), 1.0, 0.0).astype(f32)
    held = jnp.broadcast_to(held, (CAP, TOK))
    before = lax.broadcasted_iota(jnp.int32, (TOK, TOK), 0) < lax.broadcasted_iota(
        jnp.int32, (TOK, TOK), 1
    )
    rank = jnp.dot(
        held.astype(bf16), before.astype(f32).astype(bf16), preferred_element_type=f32
    )
    slot = lax.broadcasted_iota(jnp.int32, (CAP, TOK), 0).astype(f32)
    sel = jnp.where((held > 0.5) & (rank == slot), 1.0, 0.0).astype(f32)
    total = jnp.zeros((TOK, 1), f32)
    for cols in columns():
        part = cols.start // HALF
        held_cols = slice(cols.start - part * HALF, cols.stop - part * HALF)
        first = turn_of() ^ part
        acc = got_ref[first, :, held_cols].astype(f32)
        for pair in range(1, EP // 2):
            acc = acc + got_ref[2 * pair + first, :, held_cols].astype(f32)
        rounded = (x_ref[:, cols].astype(f32) + acc).astype(bf16)
        res_ref[:, cols] = rounded
        wide = rounded.astype(f32)
        total = total + jnp.sum(wide * wide, axis=-1, keepdims=True)
    factor = lax.rsqrt(total / D + norm_eps)
    for cols in columns():
        wide = res_ref[:, cols].astype(f32)
        rows = (wide * factor * gain_ref[:, cols].astype(f32)).astype(bf16)
        ffn_ref[:, cols] = rows
        slots = jnp.dot(sel.astype(bf16), rows, preferred_element_type=f32).astype(bf16)
        for dest in range(EP):
            copies_ref[dest, :, cols] = slots
    logits = dot_last(router_ref[...], ffn_ref[...])
    expert = lax.broadcasted_iota(jnp.int32, (EXPERTS, TOK), 0)
    pick_one = jnp.sum(jnp.where(expert == one, logits, 0.0), axis=0, keepdims=True)
    pick_two = jnp.sum(jnp.where(expert == two, logits, 0.0), axis=0, keepdims=True)
    top = jnp.maximum(pick_one, pick_two)
    e_one = jnp.exp(pick_one - top)
    e_two = jnp.exp(pick_two - top)
    both = e_one + e_two
    share = jnp.where(one == 0, e_one / both, 0.0) + jnp.where(two == 0, e_two / both, 0.0)
    coef_ref[...] = share * sel


def expert_body(x_ref, gate_ref, up_ref, down_ref, part_ref):
    x = x_ref[...]
    gate = dot_last(gate_ref[...], x)
    up = dot_last(up_ref[...], x)
    hidden = (gate * jax.nn.sigmoid(gate) * up).astype(bf16)
    part_ref[...] = lax.dot_general(
        hidden, down_ref[0], (((0,), (0,)), ((), ())), preferred_element_type=f32
    ).astype(bf16)


def combine_body(res_ref, coef_ref, got_ref, out_ref):
    coef = coef_ref[...]
    for cols in columns():
        acc = got_ref[0, :, cols].astype(f32)
        for src in range(1, EP):
            acc = acc + got_ref[src, :, cols].astype(f32)
        out_ref[:, cols] = (res_ref[:, cols].astype(f32) + dot_first(coef, acc)).astype(bf16)


def sds(shape, dtype):
    return jax.ShapeDtypeStruct(shape, dtype)


def trade(pieces):
    return lax.all_to_all(pieces, "ep", split_axis=0, concat_axis=0, tiled=True)


def local(
    states,
    entering,
    seq_lens,
    routes,
    attn_norm,
    ffn_norm,
    wq,
    wk,
    wv,
    wo,
    router,
    w_gate,
    w_up,
    w_down,
    cache_k,
    cache_v,
    k_scale,
    v_scale,
):
    rotary = rotary_table()
    ks = jnp.transpose(k_scale[0], (0, 2, 3, 1))
    vs = jnp.transpose(v_scale[0], (0, 2, 3, 1))
    chosen = jnp.transpose(routes[0], (0, 2, 1))
    router_t, gate_t, up_t = (
        jnp.transpose(w[0], (1, 0)) for w in (router, w_gate, w_up)
    )

    turn = turn_of()
    ep_index = lax.axis_index("ep")
    sections = lax.axis_size("section")
    sent_depth = ((ep_index >> 2) + turn + 1) % 2 * HALF
    sent_cols = (ep_index + turn + 1) % 2 * HALF
    both = ("section", "ep")
    joined = jnp.concatenate([wq[0], wk[0], wv[0]], axis=1)
    sent_wo = lax.dynamic_slice(wo[0], (0, sent_cols), (256, HALF))
    sent_qkv = lax.dynamic_slice(joined, (sent_depth, 0), (HALF, QKV))
    own_wo = lax.dynamic_slice(wo[0], (0, HALF - sent_cols), (256, HALF))
    own_qkv = lax.dynamic_slice(joined, (HALF - sent_depth, 0), (HALF, QKV))
    others = (
        lax.ppermute(sent_wo, both, partner_list("x", sections)),
        lax.ppermute(sent_qkv, both, partner_list("y", sections)),
    )

    copies = call(
        norm_body,
        sds((EP, TOK, D), bf16),
        2,
        far_out=True,
        name="norm",
        scratch=[pltpu.VMEM((TOK, D), bf16), pltpu.SemaphoreType.DMA((EP,))],
    )(states, attn_norm)
    everyone, own_wo, own_qkv = lax.optimization_barrier(
        (trade(copies).reshape(EP * TOK, D), own_wo, own_qkv)
    )
    projected = call(project_body, sds((EP * TOK, QKV), bf16), 2, name="project", limit=8)(
        everyone, joined
    )

    def run_layer(x, projected, tick, others):
        got = trade(projected.reshape(EP, TOK, projected.shape[1]))
        attended = call(
            functools.partial(attention_body, tick), sds((EP, TOK, 512), bf16), 7, name="attend"
        )(got, seq_lens, rotary, ks, vs, cache_k, cache_v)
        part = sds((EP * TOK, HALF), bf16)
        if tick == 0:
            attended, *others = lax.optimization_barrier((attended, *others))
            heads = trade(attended).reshape(EP * TOK, 512)
            part, *others = call(
                out_fetch_body,
                (part, *(sds(o.shape, bf16) for o in others)),
                4,
                far=(2, 3),
                name="outproj",
                scratch=[pltpu.SemaphoreType.DMA((2,))],
            )(heads, own_wo, *others)
        else:
            heads = trade(attended).reshape(EP * TOK, 512)
            part = call(out_body, part, 3, name="outproj")(heads, own_wo, others[0])
        sums = trade(part.reshape(EP, TOK, HALF))
        residual, slots, coef = call(
            functools.partial(residual_body, tick),
            (sds((TOK, D), bf16), sds((EP, CAP, D), bf16), sds((CAP, TOK), f32)),
            5,
            name="residual",
            scratch=[pltpu.VMEM((TOK, D), bf16)],
        )(x, sums, ffn_norm, router_t, chosen)
        landed = trade(slots).reshape(EP * CAP, D)
        pieces = call(expert_body, sds((EP * CAP, D), bf16), 4, name="expert", limit=8)(
            landed, gate_t, up_t, w_down
        )
        returned = trade(pieces.reshape(EP, CAP, D))
        out = call(combine_body, sds((TOK, D), bf16), 3, name="combine")(residual, coef, returned)
        return out, others

    first_out, others = run_layer(states, projected, 0, others)
    shifted = lax.ppermute(first_out, "section", [(i, i + 1) for i in range(sections - 1)])
    second_in, copies = call(
        norm_select_body,
        (sds((TOK, D), bf16), sds((EP, TOK, HALF), bf16)),
        3,
        name="select_norm",
    )(entering, shifted, attn_norm)
    everyone = trade(copies).reshape(EP * TOK, HALF)
    projected = call(project_halves_body, sds((EP * TOK, 2 * QKV), bf16), 3, name="project2")(
        everyone, own_qkv, others[1]
    )
    return run_layer(second_in, projected, 1, others)[0]


def solution(mesh):
    return jax.shard_map(
        local,
        mesh=mesh,
        in_specs=(
            P(("section", "ep"), None),
            P("ep", None),
            P(),
            P("section", None, "ep", None),
            P("section", None),
            P("section", None),
            P("section", None, "ep"),
            P("section", None, "ep"),
            P("section", None, "ep"),
            P("section", "ep", None),
            P("section", None, None),
            P("section", None, "ep"),
            P("section", None, "ep"),
            P("section", "ep", None),
            P("section", None, "ep", None, None, None),
            P("section", None, "ep", None, None, None),
            P("section", None, "ep", None, None),
            P("section", None, "ep", None, None),
        ),
        out_specs=P(("section", "ep"), None),
        check_vma=False,
    )
```

```python
import functools

import jax
import jax.numpy as jnp
import numpy as np
from jax import lax
from jax.experimental import pallas as pl
from jax.experimental.pallas import tpu as pltpu
from jax.sharding import PartitionSpec as P

D = 3072
QH = 32
KVH = 8
HD = 128
EXPERTS = 8
EXP_WIN = 1
LEN = 16
BLK = 4
CAP = 8
EP = 16
TOK = 16
CHUNK = 512
HALF = D // 2
QKV = 384

rope_base = 1000000.0
norm_eps = 1e-05
f32 = jnp.float32
bf16 = jnp.bfloat16


def call(body, out_shape, n_in, far=(), far_out=False, name=None, scratch=(), limit=4):
    specs = [
        pl.BlockSpec(memory_space=pl.ANY if i in far else pltpu.VMEM) for i in range(n_in)
    ]
    space = pl.ANY if far_out else pltpu.VMEM
    outs = jax.tree.map(lambda _: pl.BlockSpec(memory_space=space), out_shape)
    return pl.pallas_call(
        body,
        out_shape=out_shape,
        in_specs=specs,
        out_specs=outs,
        scratch_shapes=list(scratch),
        compiler_params=pltpu.CompilerParams(vmem_limit_bytes=limit << 20),
        name=name,
    )


def dot_last(left, right):
    return lax.dot_general(left, right, (((1,), (1,)), ((), ())), preferred_element_type=f32)


def dot_first(left, right):
    return lax.dot_general(
        left,
        right,
        (((0,), (0,)), ((), ())),
        preferred_element_type=f32,
        precision=lax.Precision.HIGHEST,
    )


def columns():
    return [slice(c, c + CHUNK) for c in range(0, D, CHUNK)]


def turn_of():
    return lax.axis_index("section") & 1


def x_partner(device, turn):
    x = device & 3
    odd = ((((x + 1) & 3) ^ 1) + 3) & 3
    return (device - x) + jnp.where(turn == 0, x ^ 1, odd)


def y_partner(device, turn):
    y = device >> 2
    odd = ((((y + 1) & 3) ^ 1) + 3) & 3
    return (device & 3) + 4 * jnp.where(turn == 0, y ^ 1, odd)


def partner_list(partner, sections):
    def odd_pair(v):
        return ((((v + 1) & 3) ^ 1) + 3) & 3

    pairs = []
    for section in range(sections):
        for device in range(EP):
            y, x = divmod(device, 4)
            if partner == "x":
                x = x ^ 1 if section % 2 == 0 else odd_pair(x)
            else:
                y = y ^ 1 if section % 2 == 0 else odd_pair(y)
            pairs.append((section * EP + device, section * EP + 4 * y + x))
    return pairs


def spread_halves(x_ref, gain_ref, copies_ref):
    total = jnp.zeros((TOK, 1), f32)
    for cols in columns():
        wide = x_ref[:, cols].astype(f32)
        total = total + jnp.sum(wide * wide, axis=-1, keepdims=True)
    factor = lax.rsqrt(total / D + norm_eps)
    turn = turn_of()
    for cols in columns():
        wide = x_ref[:, cols].astype(f32)
        rows = (wide * factor * gain_ref[:, cols].astype(f32)).astype(bf16)
        part = cols.start // HALF
        kept = slice(cols.start - part * HALF, cols.stop - part * HALF)
        for k in range(2):
            for x in range(4):
                copies_ref[(2 * k + (turn ^ part)) * 4 + x, :, kept] = rows


def norm_body(both_ref, copies_hbm, rows_ref, sems):
    x_ref = both_ref.at[0:TOK]
    gain_ref = both_ref.at[TOK : TOK + 1]
    total = jnp.zeros((TOK, 1), f32)
    for cols in columns():
        wide = x_ref[:, cols].astype(f32)
        total = total + jnp.sum(wide * wide, axis=-1, keepdims=True)
    factor = lax.rsqrt(total / D + norm_eps)
    for cols in columns():
        wide = x_ref[:, cols].astype(f32)
        rows_ref[:, cols] = (wide * factor * gain_ref[:, cols].astype(f32)).astype(bf16)
    sends = [
        pltpu.make_async_copy(rows_ref, copies_hbm.at[dest], sems.at[dest]) for dest in range(EP)
    ]
    for send in sends:
        send.start()
    for send in sends:
        send.wait()


def norm_select_body(entering_ref, shifted_ref, gain_ref, x_ref, copies_ref):
    is_first = lax.axis_index("section") == 0

    @pl.when(is_first)
    def _():
        x_ref[...] = entering_ref[...]

    @pl.when(jnp.logical_not(is_first))
    def _():
        x_ref[...] = shifted_ref[...]

    spread_halves(x_ref, gain_ref, copies_ref)


def project_body(x_ref, joined_ref, out_ref):
    out_ref[...] = jnp.dot(x_ref[...], joined_ref[...], preferred_element_type=f32).astype(bf16)


def project_halves_body(x_ref, own_ref, other_ref, out_ref):
    x = x_ref[...]
    out_ref[:, 0:QKV] = jnp.dot(x, own_ref[...], preferred_element_type=f32).astype(bf16)
    out_ref[:, QKV : 2 * QKV] = jnp.dot(x, other_ref[...], preferred_element_type=f32).astype(bf16)


def rotary_table():
    half = HD // 2
    inv_freq = rope_base ** (-np.arange(half, dtype=np.float64) * 2.0 / HD)
    angles = np.arange(2 * LEN, dtype=np.float64)[:, None] * inv_freq
    cos_vals, sin_vals = np.cos(angles), np.sin(angles)
    return np.concatenate([cos_vals, cos_vals, -sin_vals, sin_vals], axis=1).astype(np.float32)


def attention_body(
    tick, got_ref, lens_ref, rotary_ref, ks_ref, vs_ref, key_ref, value_ref, out_ref
):
    scale = HD ** (-0.5)
    group = QH // KVH
    pos = TOK * LEN
    lane = lax.broadcasted_iota(jnp.int32, (TOK, HD), 1)
    low = lane < HD // 2
    turn = turn_of()

    def rows_of(src, start, stop):
        rows = got_ref[src, :, start:stop].astype(f32)
        if tick == 1:
            other = got_ref[y_partner(src, turn), :, QKV + start : QKV + stop].astype(f32)
            rows = (rows + other).astype(bf16).astype(f32)
        return rows

    row_lens = lens_ref[pl.ds(lax.axis_index("section") + 1 - tick, 1), :].astype(f32)
    mine = lax.broadcasted_iota(jnp.int32, (TOK, row_lens.shape[1]), 0) + lax.axis_index("ep") * TOK
    there = lax.broadcasted_iota(jnp.int32, (TOK, row_lens.shape[1]), 1)
    lens = jnp.sum(jnp.where(mine == there, row_lens, 0.0), axis=-1, keepdims=True)
    lens = lens.astype(jnp.int32)
    length = lax.broadcasted_iota(jnp.int32, (TOK, 2 * LEN), 1)
    rotary = jnp.dot(
        jnp.where(length == lens, 1.0, 0.0).astype(f32),
        rotary_ref[...],
        preferred_element_type=f32,
        precision=lax.Precision.HIGHEST,
    )
    cos_vals = rotary[:, 0:HD]
    sin_vals = rotary[:, HD : 2 * HD]

    def turned(rows):
        return (rows * cos_vals + pltpu.roll(rows, HD // 2, 1) * sin_vals).astype(bf16)

    blocks = LEN // BLK
    eye = lax.broadcasted_iota(jnp.int32, (KVH * blocks, KVH * blocks), 0)
    eye = (eye == lax.broadcasted_iota(jnp.int32, (KVH * blocks, KVH * blocks), 1)).astype(f32)
    k_rows = dot_first(jnp.concatenate([ks_ref[tick, g] for g in range(KVH)], axis=0), eye)
    v_rows = dot_first(jnp.concatenate([vs_ref[tick, g] for g in range(KVH)], axis=0), eye)
    block_at = lane % LEN // BLK

    def spread(rows, g):
        wide = jnp.broadcast_to(rows[:, g * blocks : g * blocks + 1], (TOK, HD))
        for k in range(1, blocks):
            at = g * blocks + k
            wide = jnp.where(block_at == k, rows[:, at : at + 1], wide)
        one = jnp.concatenate([wide] * (pos // HD), axis=1)
        return jnp.concatenate([one] * group, axis=0)

    row = lax.broadcasted_iota(jnp.int32, (TOK, pos), 0)
    col = lax.broadcasted_iota(jnp.int32, (TOK, pos), 1)
    live_one = (col // LEN == row) & (col % LEN < lens)
    live = jnp.concatenate([live_one.astype(f32)] * group, axis=0) > 0.5
    heads = range(KVH)
    queries, fresh_keys, fresh_values, scores = [], [], [], []
    for g in heads:
        first = rows_of(2 * g, 256, QKV)
        second = rows_of(2 * g + 1, 256, QKV)
        key_new = turned(jnp.where(low, first, pltpu.roll(second, HD // 2, 1))).astype(f32)
        fresh_keys.append(key_new)
        fresh_values.append(jnp.where(low, pltpu.roll(first, HD // 2, 1), second))
        q = jnp.concatenate(
            [
                turned(rows_of(2 * g + r // 2, (r % 2) * HD, (r % 2 + 1) * HD))
                for r in range(group)
            ],
            axis=0,
        )
        queries.append(q)
        scores.append(dot_last(q, key_ref[0, tick, :, g].reshape(pos, HD)))
    weights, owns, denoms = [], [], []
    for g in heads:
        score = jnp.where(live, scores[g] * spread(k_rows, g) * scale, -1e30)
        own = (
            jnp.sum(
                queries[g].astype(f32) * jnp.concatenate([fresh_keys[g]] * group, axis=0),
                axis=-1,
                keepdims=True,
            )
            * scale
        )
        top = jnp.maximum(jnp.max(score, axis=-1, keepdims=True), own)
        e = jnp.where(live, jnp.exp(score - top), 0.0)
        e_own = jnp.exp(own - top)
        owns.append(e_own)
        denoms.append(jnp.sum(e, axis=-1, keepdims=True) + e_own)
        weights.append((e * spread(v_rows, g)).astype(bf16))
    mixes = [
        jnp.dot(
            weights[g], value_ref[0, tick, :, g].reshape(pos, HD), preferred_element_type=f32
        )
        for g in heads
    ]
    for g in heads:
        mixed = mixes[g] + owns[g] * jnp.concatenate([fresh_values[g]] * group, axis=0)
        done = (mixed / denoms[g]).astype(bf16)
        for r in range(group):
            rows = done[r * TOK : (r + 1) * TOK]
            at = (r % 2) * HD
            owner = 2 * g + r // 2
            out_ref[owner, :, at : at + HD] = rows
            out_ref[x_partner(owner, turn), :, 256 + at : 256 + at + HD] = rows


def out_body(att_ref, wo_ref, other_ref, part_ref):
    total = jnp.dot(att_ref[:, 0:256], wo_ref[...], preferred_element_type=f32)
    total = total + jnp.dot(att_ref[:, 256:512], other_ref[...], preferred_element_type=f32)
    part_ref[...] = total.astype(bf16)


def out_fetch_body(att_ref, wo_ref, *refs):
    swapped, part_ref, fetched, sems = refs[:2], refs[2], refs[3:5], refs[5]
    fetches = [
        pltpu.make_async_copy(there, here, sems.at[i])
        for i, (there, here) in enumerate(zip(swapped, fetched))
    ]
    for fetch in fetches:
        fetch.start()
    fetches[0].wait()
    out_body(att_ref, wo_ref, fetched[0], part_ref)
    for fetch in fetches[1:]:
        fetch.wait()


def residual_body(
    tick, x_ref, got_ref, gain_ref, router_ref, chosen_ref, res_ref, copies_ref, coef_ref, ffn_ref
):
    one = chosen_ref[tick, 0:1, :]
    two = chosen_ref[tick, 1:2, :]
    held = jnp.where((one == 0) | (two == 0), 1.0, 0.0).astype(f32)
    held = jnp.broadcast_to(held, (CAP, TOK))
    before = lax.broadcasted_iota(jnp.int32, (TOK, TOK), 0) < lax.broadcasted_iota(
        jnp.int32, (TOK, TOK), 1
    )
    rank = jnp.dot(
        held.astype(bf16), before.astype(f32).astype(bf16), preferred_element_type=f32
    )
    slot = lax.broadcasted_iota(jnp.int32, (CAP, TOK), 0).astype(f32)
    sel = jnp.where((held > 0.5) & (rank == slot), 1.0, 0.0).astype(f32)
    total = jnp.zeros((TOK, 1), f32)
    for cols in columns():
        part = cols.start // HALF
        held_cols = slice(cols.start - part * HALF, cols.stop - part * HALF)
        first = turn_of() ^ part
        acc = got_ref[first, :, held_cols].astype(f32)
        for pair in range(1, EP // 2):
            acc = acc + got_ref[2 * pair + first, :, held_cols].astype(f32)
        rounded = (x_ref[:, cols].astype(f32) + acc).astype(bf16)
        res_ref[:, cols] = rounded
        wide = rounded.astype(f32)
        total = total + jnp.sum(wide * wide, axis=-1, keepdims=True)
    factor = lax.rsqrt(total / D + norm_eps)
    for cols in columns():
        wide = res_ref[:, cols].astype(f32)
        rows = (wide * factor * gain_ref[:, cols].astype(f32)).astype(bf16)
        ffn_ref[:, cols] = rows
        slots = jnp.dot(sel.astype(bf16), rows, preferred_element_type=f32).astype(bf16)
        for dest in range(EP):
            copies_ref[dest, :, cols] = slots
    logits = dot_last(router_ref[...], ffn_ref[...])
    expert = lax.broadcasted_iota(jnp.int32, (EXPERTS, TOK), 0)
    pick_one = jnp.sum(jnp.where(expert == one, logits, 0.0), axis=0, keepdims=True)
    pick_two = jnp.sum(jnp.where(expert == two, logits, 0.0), axis=0, keepdims=True)
    top = jnp.maximum(pick_one, pick_two)
    e_one = jnp.exp(pick_one - top)
    e_two = jnp.exp(pick_two - top)
    both = e_one + e_two
    share = jnp.where(one == 0, e_one / both, 0.0) + jnp.where(two == 0, e_two / both, 0.0)
    coef_ref[...] = share * sel


def expert_body(x_ref, gate_ref, up_ref, down_ref, part_ref):
    x = x_ref[...]
    gate = dot_last(gate_ref[...], x)
    up = dot_last(up_ref[...], x)
    hidden = (gate * jax.nn.sigmoid(gate) * up).astype(bf16)
    part_ref[...] = lax.dot_general(
        hidden, down_ref[0], (((0,), (0,)), ((), ())), preferred_element_type=f32
    ).astype(bf16)


def combine_body(res_ref, coef_ref, got_ref, out_ref):
    coef = coef_ref[...]
    for cols in columns():
        acc = got_ref[0, :, cols].astype(f32)
        for src in range(1, EP):
            acc = acc + got_ref[src, :, cols].astype(f32)
        out_ref[:, cols] = (res_ref[:, cols].astype(f32) + dot_first(coef, acc)).astype(bf16)


def sds(shape, dtype):
    return jax.ShapeDtypeStruct(shape, dtype)


def trade(pieces):
    return lax.all_to_all(pieces, "ep", split_axis=0, concat_axis=0, tiled=True)


def local(
    states,
    entering,
    seq_lens,
    routes,
    attn_norm,
    ffn_norm,
    wq,
    wk,
    wv,
    wo,
    router,
    w_gate,
    w_up,
    w_down,
    cache_k,
    cache_v,
    k_scale,
    v_scale,
):
    rotary = rotary_table()
    ks = jnp.transpose(k_scale[0], (0, 2, 3, 1))
    vs = jnp.transpose(v_scale[0], (0, 2, 3, 1))
    chosen = jnp.transpose(routes[0], (0, 2, 1))
    router_t, gate_t, up_t = (
        jnp.transpose(w[0], (1, 0)) for w in (router, w_gate, w_up)
    )

    turn = turn_of()
    ep_index = lax.axis_index("ep")
    sections = lax.axis_size("section")
    sent_depth = ((ep_index >> 2) + turn + 1) % 2 * HALF
    sent_cols = (ep_index + turn + 1) % 2 * HALF
    both = ("section", "ep")
    joined = jnp.concatenate([wq[0], wk[0], wv[0]], axis=1)
    sent_wo = lax.dynamic_slice(wo[0], (0, sent_cols), (256, HALF))
    sent_qkv = lax.dynamic_slice(joined, (sent_depth, 0), (HALF, QKV))
    own_wo = lax.dynamic_slice(wo[0], (0, HALF - sent_cols), (256, HALF))
    own_qkv = lax.dynamic_slice(joined, (HALF - sent_depth, 0), (HALF, QKV))
    others = (
        lax.ppermute(sent_wo, both, partner_list("x", sections)),
        lax.ppermute(sent_qkv, both, partner_list("y", sections)),
    )

    copies = call(
        norm_body,
        sds((EP, TOK, D), bf16),
        1,
        far_out=True,
        name="norm",
        scratch=[pltpu.VMEM((TOK, D), bf16), pltpu.SemaphoreType.DMA((EP,))],
    )(jnp.concatenate([states, attn_norm], axis=0))
    everyone, own_wo, own_qkv = lax.optimization_barrier(
        (trade(copies).reshape(EP * TOK, D), own_wo, own_qkv)
    )
    projected = call(project_body, sds((EP * TOK, QKV), bf16), 2, name="project", limit=8)(
        everyone, joined
    )

    def run_layer(x, projected, tick, others):
        got = trade(projected.reshape(EP, TOK, projected.shape[1]))
        attended = call(
            functools.partial(attention_body, tick), sds((EP, TOK, 512), bf16), 7, name="attend"
        )(got, seq_lens, rotary, ks, vs, cache_k, cache_v)
        part = sds((EP * TOK, HALF), bf16)
        if tick == 0:
            attended, *others = lax.optimization_barrier((attended, *others))
            heads = trade(attended).reshape(EP * TOK, 512)
            part, *others = call(
                out_fetch_body,
                (part, *(sds(o.shape, bf16) for o in others)),
                4,
                far=(2, 3),
                name="outproj",
                scratch=[pltpu.SemaphoreType.DMA((2,))],
            )(heads, own_wo, *others)
        else:
            heads = trade(attended).reshape(EP * TOK, 512)
            part = call(out_body, part, 3, name="outproj")(heads, own_wo, others[0])
        sums = trade(part.reshape(EP, TOK, HALF))
        residual, slots, coef = call(
            functools.partial(residual_body, tick),
            (sds((TOK, D), bf16), sds((EP, CAP, D), bf16), sds((CAP, TOK), f32)),
            5,
            name="residual",
            scratch=[pltpu.VMEM((TOK, D), bf16)],
        )(x, sums, ffn_norm, router_t, chosen)
        landed = trade(slots).reshape(EP * CAP, D)
        pieces = call(expert_body, sds((EP * CAP, D), bf16), 4, name="expert", limit=8)(
            landed, gate_t, up_t, w_down
        )
        returned = trade(pieces.reshape(EP, CAP, D))
        out = call(combine_body, sds((TOK, D), bf16), 3, name="combine")(residual, coef, returned)
        return out, others

    first_out, others = run_layer(states, projected, 0, others)
    shifted = lax.ppermute(first_out, "section", [(i, i + 1) for i in range(sections - 1)])
    second_in, copies = call(
        norm_select_body,
        (sds((TOK, D), bf16), sds((EP, TOK, HALF), bf16)),
        3,
        name="select_norm",
    )(entering, shifted, attn_norm)
    everyone = trade(copies).reshape(EP * TOK, HALF)
    projected = call(project_halves_body, sds((EP * TOK, 2 * QKV), bf16), 3, name="project2")(
        everyone, own_qkv, others[1]
    )
    return run_layer(second_in, projected, 1, others)[0]


def solution(mesh):
    return jax.shard_map(
        local,
        mesh=mesh,
        in_specs=(
            P(("section", "ep"), None),
            P("ep", None),
            P(),
            P("section", None, "ep", None),
            P("section", None),
            P("section", None),
            P("section", None, "ep"),
            P("section", None, "ep"),
            P("section", None, "ep"),
            P("section", "ep", None),
            P("section", None, None),
            P("section", None, "ep"),
            P("section", None, "ep"),
            P("section", "ep", None),
            P("section", None, "ep", None, None, None),
            P("section", None, "ep", None, None, None),
            P("section", None, "ep", None, None),
            P("section", None, "ep", None, None),
        ),
        out_specs=P(("section", "ep"), None),
        check_vma=False,
    )
```
